32 devices in a mesh: cuts: 2 (over x), rows: 16 (over z, y, core).
Axes of the slice: x: 2, y: 2, z: 4, core: 2. Of those that a mesh axis runs over, the one named last changes fastest.
Arguments:
- start_modes: float32 [2, 64, 512, 128], P('cuts', 'rows'), may hold values from -6 to 6
- contrast: float32 [2, 64, 512], P('cuts', 'rows'), may hold values from 0 to 1
- rotations: float32 [2, 2, 128, 128], P('cuts'), may hold values from -0.2 to 1.2, as said below
- ordering: int32 [2, 2, 128], P('cuts'), may hold values from 0 to 127, each once within a row
Outputs:
- modes: float32 [2, 64, 512, 128], P('cuts', 'rows')
- coupling: float32 [2, 128, 128], P('cuts', 'rows')
- rayleigh: float32 [2, 128, 128], P('cuts', 'rows')
The draws below stay inside these ranges and needn't reach their ends.
Inputs may be any that keep to these rules, and one draw needn't show every extreme that they name: `rotations`: each matrix is invertible.
All inputs are finite; a program needn't handle non-finite values.
Results may differ from the reference program's by a relative error of at most 0.00026.
Values sent between devices are 32-bit elements; how exact they have to be, the bound alone decides.
No kernel may reach another device: no remote copies, remote signals or barrier semaphores. Data moves between devices by JAX's collectives and lax.ppermute only.
A program may use at most 64 MiB of HBM per device.

```python
import math
import jax
import jax.numpy as jnp
from jax import lax

MODES = 128
DEGREE = 4
ITERS = 2
GC = 512
SLICES = 2
GR = 64


def draw_rotations(key, part):
    spread = 0.3 / math.sqrt(MODES)
    shape = (SLICES, ITERS, MODES, MODES)
    noise = jax.random.truncated_normal(key, -4.0, 4.0, shape, jnp.float32) * spread
    identity = (jnp.arange(MODES)[:, None] == jnp.arange(MODES)[None, :]).astype(jnp.float32)
    return identity + noise


def block_levels(own_key, extent, split, smallest, high):
    level, own = 1.0, jax.random.fold_in(own_key, 6)
    for position, shards_of in split:
        heights = jnp.exp(jax.random.uniform(jax.random.fold_in(own, position), (shards_of,), jnp.float32, smallest / len(split), high / len(split)))
        level = level * jnp.repeat(heights, extent[position] // shards_of).reshape([-1 if axis == position else 1 for axis in range(len(extent))])
    return level


def bell_draw(stream_key, dims, scale, limit, split=(), kind=jnp.bfloat16):
    entries = scale * jax.random.normal(stream_key, dims, jnp.float32)
    if split:
        entries = entries * block_levels(stream_key, dims, split, -0.22, 0.18)
    return jnp.clip(entries, -limit, limit).astype(kind)


def setup_inputs(seed: int = 0) -> dict:
    key_list = jax.random.split(jax.random.key(seed), 5)
    return {
        "start_modes": bell_draw(key_list[0], (SLICES, GR, GC, MODES), 1.0, 6.0, ((0, 2), (1, 16)), jnp.float32),
        "contrast": jnp.clip(1.0 * jax.random.uniform(key_list[1], (SLICES, GR, GC), jnp.float32) ** block_levels(key_list[1], (SLICES, GR, GC), ((0, 2), (1, 16)), -0.2, 0.2), 0.0, 1.0),
        "rotations": draw_rotations(jax.random.fold_in(key_list[4], 71), 0),
        "ordering": jax.vmap(lambda own: jax.random.permutation(own, MODES))(jax.random.split(key_list[3], SLICES * ITERS)).reshape((SLICES, ITERS, MODES)).astype(jnp.int32),
    }


def neighbour_sum(center, rows_source):
    columns = jnp.pad(center, ((0, 0), (1, 1), (0, 0)))
    return rows_source[2:] + rows_source[:-2] + columns[:, 2:] + columns[:, :-2]

def operator_core(center, rows_source, section):
    return 0.8 * (section[:, :, None] * center + 0.25 * neighbour_sum(center, rows_source)) - 0.2 * center

def inner_modes(left, right):
    return jnp.einsum('rcm,rcn->mn', left, right, precision=lax.Precision.HIGHEST)

def reference(start_modes, contrast, rotations, ordering):
    pixels = GR * GC
    all_modes = []
    all_coupling = []
    all_rayleigh = []
    earlier = start_modes[0]
    for slice_id in range(SLICES):
        section = contrast[slice_id]
        subspace = start_modes[slice_id]

        def apply_full(vectors):
            return operator_core(vectors, jnp.pad(vectors, ((1, 1), (0, 0), (0, 0))), section)
        for sweep in range(ITERS):
            before = subspace
            current = apply_full(before)
            for degree_step in range(2, DEGREE + 1):
                following = 2.0 * apply_full(current) - before
                before, current = (current, following)
            filtered = current
            gram_sum = inner_modes(filtered, filtered) / pixels
            factor_low = jnp.linalg.cholesky(gram_sum)
            mixing = lax.linalg.triangular_solve(factor_low, rotations[slice_id, sweep], left_side=True, lower=True, transpose_a=True)
            picker = (ordering[slice_id, sweep][None, :] == jnp.arange(MODES, dtype=jnp.int32)[:, None]).astype(jnp.float32)
            mixing = jnp.dot(mixing, picker, precision=lax.Precision.HIGHEST)
            subspace = jnp.einsum('rcm,mn->rcn', filtered, mixing, precision=lax.Precision.HIGHEST)
        applied = apply_full(subspace)
        all_coupling.append(inner_modes(earlier, subspace) / pixels)
        all_rayleigh.append(inner_modes(subspace, applied) / pixels)
        all_modes.append(subspace)
        earlier = subspace
    return (jnp.stack(all_modes), jnp.stack(all_coupling), jnp.stack(all_rayleigh))
```

```python
import functools

import jax
import jax.numpy as jnp
from jax import lax
from jax.experimental import pallas as pl
from jax.experimental.pallas import tpu as pltpu
from jax.sharding import PartitionSpec as P

DEGREE = 4
ITERS = 2
DEPTH = DEGREE * ITERS
LANES = 128
HIGHEST = lax.Precision.HIGHEST


def mm(a, b):
    return jnp.dot(a, b, precision=HIGHEST, preferred_element_type=jnp.float32)


def mm_t(a, b):
    return lax.dot_general(
        a, b, (((0,), (0,)), ((), ())), precision=HIGHEST, preferred_element_type=jnp.float32
    )


def filter_kernel(
    dims, pos, *refs
):
    rows_here, group, wide, core = dims
    n_msg = 2 * group
    tall = rows_here * group
    total = tall + 2 * DEPTH
    messages, refs = refs[:n_msg], refs[n_msg:]
    gram1, gram2, ray, coup, out, x, y, weight, start, cs, tmp, sem, sem2 = refs
    span = wide + 2 * DEPTH
    left = DEPTH
    core_at = left + DEPTH
    col = pl.multiple_of(pos[n_msg], 8)
    low, high = pos[n_msg + 1], pos[n_msg + 2]
    at_left, at_right = pos[n_msg + 3], pos[n_msg + 4]
    first = pos[n_msg + 5]
    nm = x.shape[2]
    zero = jnp.zeros((16, nm), jnp.float32)

    def clear(r, _):
        for buf in (x, y, weight):
            buf[r, 0:16, :] = zero
            buf[r, span - 16 : span, :] = zero
        return 0

    lax.fori_loop(0, total, clear, 0)
    blank = jnp.zeros((span, nm), jnp.float32)
    y[DEPTH - 1] = blank
    y[DEPTH + tall] = blank
    copies = []
    for i, message in enumerate(messages):
        row = pos[i]
        for r in range(rows_here):
            copies.append(
                pltpu.make_async_copy(
                    message.at[pl.ds(r * wide, wide), :],
                    x.at[row + r, pl.ds(col, wide), :],
                    sem.at[i, r],
                )
            )
        copies.append(
            pltpu.make_async_copy(
                message.at[pl.ds(rows_here * wide, 2 * rows_here), :],
                cs.at[pl.ds(pl.multiple_of(2 * row, 2 * rows_here), 2 * rows_here), :],
                sem.at[i, rows_here],
            )
        )
    for c in copies:
        c.start()
    for c in copies:
        c.wait()
    turned = (1.6 * cs[...] - 0.4).T
    for r in range(total):
        weight[r, pl.ds(col, LANES), :] = jnp.broadcast_to(
            turned[:, 2 * r : 2 * r + 1], (LANES, nm)
        )
        weight[r, pl.ds(pl.multiple_of(col + LANES, 8), wide - LANES), :] = jnp.broadcast_to(
            turned[: wide - LANES, 2 * r + 1 : 2 * r + 2], (wide - LANES, nm)
        )
    keep = pltpu.make_async_copy(
        x.at[pl.ds(DEPTH, tall), pl.ds(core_at, core), :], start, sem2
    )
    keep.start()
    keep.wait()

    def apply(dst, src, k, opening):
        def row(r, _):
            ctr = src[r, left : left + wide, :]
            s = (src[r - 1, left : left + wide, :] + src[r + 1, left : left + wide, :]) + (
                src[r, left - 1 : left - 1 + wide, :] + src[r, left + 1 : left + 1 + wide, :]
            )
            v = weight[r, left : left + wide, :] * ctr + 0.4 * s
            if opening:
                v = 0.5 * v
            else:
                v = v - dst[r, left : left + wide, :]
            edge = v[0:DEPTH]
            dst[r, left : left + DEPTH, :] = jnp.where(at_left == 1, jnp.zeros_like(edge), edge)
            dst[r, left + DEPTH : left + wide - DEPTH, :] = v[DEPTH : wide - DEPTH]
            edge = v[wide - DEPTH :]
            dst[r, left + wide - DEPTH : left + wide, :] = jnp.where(
                at_right == 1, jnp.zeros_like(edge), edge
            )
            return 0

        lax.fori_loop(jnp.maximum(low, k), jnp.minimum(high, total - k), row, 0)

    def gram(dst, a, b):
        dst[...] = jnp.zeros_like(dst)

        def chunk(i, _):
            dst[...] += mm_t(a(i), b(i))
            return 0

        lax.fori_loop(0, tall // rows_here, chunk, 0)

    def core_rows(buf, at):
        def take(i):
            base = at + i * rows_here
            return buf[pl.ds(base, rows_here), core_at : core_at + core, :].reshape(
                rows_here * core, nm
            )

        return take

    for sweep in range(ITERS):
        for step in range(1, DEGREE + 1):
            k = sweep * DEGREE + step
            dst, src = (y, x) if step % 2 else (x, y)
            apply(dst, src, k, step == 1)
        if sweep == 0:
            gram(gram1, core_rows(x, DEPTH), core_rows(x, DEPTH))
    gram(gram2, core_rows(x, DEPTH), core_rows(x, DEPTH))

    c0, c1 = core_at, core_at + core

    def half(i, _):
        r = DEPTH + i
        ctr = x[r, c0:c1, :]
        right = x[r, c0 + 1 : c1 + 1, :]
        spot = lax.broadcasted_iota(jnp.int32, (core, nm), 0)
        right = jnp.where(spot == core - 1, 0.0, right)
        down = x[r + 1, c0:c1, :]
        down = jnp.where(i == tall - 1, jnp.zeros_like(down), down)
        tmp[i] = 0.25 * weight[r, c0:c1, :] * ctr + 0.2 * (right + down)
        out[i] = ctr
        return 0

    lax.fori_loop(0, tall, half, 0)

    def plain(buf):
        def take(i):
            return buf[pl.ds(i * rows_here, rows_here)].reshape(rows_here * core, nm)

        return take

    gram(ray, plain(out), plain(tmp))

    @pl.when(first == 1)
    def _():
        gram(coup, plain(start), plain(out))

    @pl.when(first != 1)
    def _():
        coup[...] = jnp.zeros_like(coup)


def late_kernel(dims, out, recv, down, right, ray0, coup0, ray, coup):
    rows_here, tall, core = dims
    nm = out.shape[2]
    coup[...] = coup0[...]

    def chunk(i, _):
        a = recv[pl.ds(i * rows_here, rows_here)].reshape(rows_here * core, nm)
        b = out[pl.ds(i * rows_here, rows_here)].reshape(rows_here * core, nm)
        coup[...] += mm_t(a, b)
        return 0

    lax.fori_loop(0, tall // rows_here, chunk, 0)
    side = out[:, core - 1, :]
    ray[...] = ray0[...] + 0.2 * (mm_t(out[tall - 1], down[0]) + mm_t(side, right[:, 0, :]))


def modes_kernel(dims, pos, *refs):
    rows_here, group, core = dims
    own, others, mix, modes = refs[0], refs[1:group], refs[group], refs[group + 1]
    nm = mix.shape[0]
    m = mix[...]
    first = pos[0] * rows_here
    for r in range(rows_here):
        modes[r, pl.ds(pl.multiple_of(pos[0] * core, core), core), :] = mm(own[first + r], m)
        for k in range(1, group):
            modes[r, pl.ds(pl.multiple_of(pos[k] * core, core), core), :] = mm(
                others[k - 1][r], m
            )


def xor_swap(value, axis, bit):
    peers = lax.axis_size(axis)
    return lax.ppermute(value, axis, [(i, i ^ bit) for i in range(peers)])


def sum_pair(one, two, axis):
    peers = lax.axis_size(axis)
    odd = (lax.axis_index(axis) & 1) == 1
    mine = jnp.where(odd, two, one) + xor_swap(jnp.where(odd, one, two), axis, 1)
    bit = 2
    while bit < peers:
        mine = mine + xor_swap(mine, axis, bit)
        bit *= 2
    other = xor_swap(mine, axis, 1)
    return jnp.where(odd, other, mine), jnp.where(odd, mine, other)


def body(start_modes, contrast, rotations, ordering):
    v0, section = start_modes[0], contrast[0]
    rows_here, columns, nm = v0.shape
    peers = lax.axis_size("rows")
    cuts = lax.axis_size("cuts")
    near = DEPTH // rows_here
    group = 2 * near
    core = columns // group
    wide = core + 2 * DEPTH
    tall = group * rows_here
    pixels = rows_here * peers * columns
    me = lax.axis_index("rows")
    cut = lax.axis_index("cuts")
    q = me % group
    block = me // group
    blocks = peers // group

    def window(k):
        at = jnp.clip((q ^ k) * core - DEPTH, 0, columns - wide)
        part = lax.dynamic_slice(v0, (0, at, 0), (rows_here, wide, nm)).reshape(-1, nm)
        tail = lax.dynamic_slice(section, (0, at), (rows_here, wide))
        tail = jnp.pad(tail, ((0, 0), (0, 2 * LANES - wide))).reshape(2 * rows_here, LANES)
        return jnp.concatenate([part, tail], axis=0)

    def hop(j, relayed=False):
        pairs = []
        for i in range(peers):
            z, s = i // group, i % group
            to = z + 1 if (s >= near) != relayed else z - 1
            if 0 <= to < blocks:
                pairs.append((i, to * group + (s ^ j)))
        return pairs

    windows = [window(k) for k in range(group)]
    arrived = [None] * group
    for k in reversed(range(1, group)):
        arrived[k] = xor_swap(windows[k], "rows", k)
    direct = [lax.ppermute(windows[j], "rows", hop(j)) for j in range(near)]
    relay = [lax.ppermute(arrived[k], "rows", hop(0, True)) for k in range(near, group)]
    messages = [windows[0]] + arrived[1:] + direct + relay

    lower = q >= near
    place = [DEPTH + (q ^ k) * rows_here for k in range(group)]
    for j in range(near):
        source = q ^ j
        place.append(
            jnp.where(lower, (source - near) * rows_here, DEPTH + tall + source * rows_here)
        )
    for k in range(near, group):
        source = q ^ k
        place.append(
            jnp.where(lower, DEPTH + tall + source * rows_here, (source - near) * rows_here)
        )
    at = jnp.clip(q * core - DEPTH, 0, columns - wide)
    place.append(DEPTH + at - (q * core - DEPTH))
    place.append(jnp.where(block == 0, DEPTH, 0))
    place.append(jnp.where(block == blocks - 1, DEPTH + tall, 2 * DEPTH + tall))
    place.append((q == 0).astype(jnp.int32))
    place.append((q == group - 1).astype(jnp.int32))
    place.append((cut == 0).astype(jnp.int32))
    place = jnp.stack([jnp.asarray(p, jnp.int32) for p in place])

    square = jax.ShapeDtypeStruct((nm, nm), jnp.float32)
    tile = jax.ShapeDtypeStruct((tall, core, nm), jnp.float32)
    total = tall + 2 * DEPTH
    span = wide + 2 * DEPTH
    vmem = pl.BlockSpec(memory_space=pltpu.VMEM)
    smem = pl.BlockSpec(memory_space=pltpu.SMEM)
    gram1, gram2, ray, coup, field = pl.pallas_call(
        functools.partial(filter_kernel, (rows_here, group, wide, core)),
        out_shape=(square, square, square, square, tile),
        in_specs=[smem] + [pl.BlockSpec(memory_space=pl.ANY)] * (2 * group),
        out_specs=[vmem] * 5,
        scratch_shapes=[
            pltpu.VMEM((total, span, nm), jnp.float32),
            pltpu.VMEM((total, span, nm), jnp.float32),
            pltpu.VMEM((total, span, nm), jnp.float32),
            pltpu.VMEM((tall, core, nm), jnp.float32),
            pltpu.VMEM((2 * total, LANES), jnp.float32),
            pltpu.VMEM((tall, core, nm), jnp.float32),
            pltpu.SemaphoreType.DMA((2 * group, rows_here + 1)),
            pltpu.SemaphoreType.DMA,
        ],
        compiler_params=pltpu.CompilerParams(vmem_limit_bytes=32 * 1024 * 1024),
        name="filters",
    )(place, *messages)

    recv = lax.ppermute(field, "cuts", [(i, i + 1) for i in range(cuts - 1)])
    down = lax.ppermute(field[:1], "rows", [(i + group, i) for i in range(peers - group)])
    right = lax.ppermute(
        field[:, :1], "rows", [(i + 1, i) for i in range(peers) if i % group != group - 1]
    )
    back = []
    for k in range(1, group):
        part = lax.dynamic_slice_in_dim(field, (q ^ k) * rows_here, rows_here, 0)
        back.append(xor_swap(part, "rows", k))

    gram1, gram2 = sum_pair(gram1, gram2, "rows")
    gram1, gram2 = gram1 / pixels, gram2 / pixels

    def mixed(g, sweep):
        low = jnp.linalg.cholesky(g)
        mix = lax.linalg.triangular_solve(
            low, rotations[0, sweep], left_side=True, lower=True, transpose_a=True
        )
        pick = (ordering[0, sweep][None, :] == jnp.arange(nm, dtype=jnp.int32)[:, None]).astype(
            jnp.float32
        )
        return mm(mix, pick)

    mix1 = mixed(gram1, 0)
    mix2 = mixed(mm(mix1.T, mm(gram2, mix1)), 1)
    mix = mm(mix1, mix2)

    ray, coup = pl.pallas_call(
        functools.partial(late_kernel, (rows_here, tall, core)),
        out_shape=(square, square),
        in_specs=[vmem] * 6,
        out_specs=[vmem] * 2,
        name="late",
    )(field, recv, down, right, ray, coup)
    ray, coup = sum_pair(ray, coup, "rows")

    before = lax.ppermute(mix, "cuts", [(i, i + 1) for i in range(cuts - 1)])
    eye = (jnp.arange(nm)[:, None] == jnp.arange(nm)[None, :]).astype(jnp.float32)
    before = jnp.where(cut == 0, eye, before)
    share = nm // peers
    mine = me * share
    left = lax.dynamic_slice_in_dim(before, mine, share, 1)
    coupling = mm(mm(left.T, coup), mix) / pixels
    left = lax.dynamic_slice_in_dim(mix, mine, share, 1)
    rayleigh = mm(mm(left.T, ray + ray.T), mix) / pixels

    where = jnp.stack([q ^ k for k in range(group)]).astype(jnp.int32)
    modes = pl.pallas_call(
        functools.partial(modes_kernel, (rows_here, group, core)),
        out_shape=jax.ShapeDtypeStruct((rows_here, columns, nm), jnp.float32),
        in_specs=[smem] + [vmem] * (group + 1),
        out_specs=vmem,
        name="modes",
    )(where, field, *back, mix)
    return modes[None], coupling[None], rayleigh[None]


def solution(mesh):
    placed = (
        P("cuts", "rows", None, None),
        P("cuts", "rows", None),
        P("cuts", None, None, None),
        P("cuts", None, None),
    )
    return jax.shard_map(
        body,
        mesh=mesh,
        in_specs=placed,
        out_specs=(P("cuts", "rows", None, None), P("cuts", "rows", None), P("cuts", "rows", None)),
        check_vma=False,
    )
```

```python
import functools

import jax
import jax.numpy as jnp
from jax import lax
from jax.experimental import pallas as pl
from jax.experimental.pallas import tpu as pltpu
from jax.sharding import PartitionSpec as P

DEGREE = 4
ITERS = 2
DEPTH = DEGREE * ITERS
LANES = 128
HIGHEST = lax.Precision.HIGHEST


def mm(a, b):
    return jnp.dot(a, b, precision=HIGHEST, preferred_element_type=jnp.float32)


def mm_t(a, b):
    return lax.dot_general(
        a, b, (((0,), (0,)), ((), ())), precision=HIGHEST, preferred_element_type=jnp.float32
    )


def spread(messages, dims, pos, col, at, sign, x, weight, cs):
    rows_here, wide = dims
    nm = x.shape[2]
    for i, message in enumerate(messages):
        for r in range(rows_here):
            x[pos[at + i] + sign * r, pl.ds(col, wide), :] = message[r * wide : (r + 1) * wide, :]
        cs[2 * rows_here * i : 2 * rows_here * (i + 1), :] = message[rows_here * wide :, :]
    turned = (1.6 * cs[...] - 0.4).T
    for i in range(len(messages)):
        for r in range(rows_here):
            row = pos[at + i] + sign * r
            c = 2 * (rows_here * i + r)
            weight[row, pl.ds(col, LANES), :] = jnp.broadcast_to(
                turned[:, c : c + 1], (LANES, nm)
            )
            weight[row, pl.ds(pl.multiple_of(col + LANES, 8), wide - LANES), :] = (
                jnp.broadcast_to(turned[: wide - LANES, c + 1 : c + 2], (wide - LANES, nm))
            )


def apply_rows(dst, src, weight, wide, sides, first, last, opening):
    left = DEPTH
    at_left, at_right = sides

    def row(r, _):
        ctr = src[r, left : left + wide, :]
        s = (src[r - 1, left : left + wide, :] + src[r + 1, left : left + wide, :]) + (
            src[r, left - 1 : left - 1 + wide, :] + src[r, left + 1 : left + 1 + wide, :]
        )
        v = weight[r, left : left + wide, :] * ctr + 0.4 * s
        if opening:
            v = 0.5 * v
        else:
            v = v - dst[r, left : left + wide, :]
        edge = v[0:DEPTH]
        dst[r, left : left + DEPTH, :] = jnp.where(at_left == 1, jnp.zeros_like(edge), edge)
        dst[r, left + DEPTH : left + wide - DEPTH, :] = v[DEPTH : wide - DEPTH]
        edge = v[wide - DEPTH :]
        dst[r, left + wide - DEPTH : left + wide, :] = jnp.where(
            at_right == 1, jnp.zeros_like(edge), edge
        )
        return 0

    lax.fori_loop(first, last, row, 0)


def block_rows(buf, at, step, lanes_at, core):
    nm = buf.shape[2]

    def take(i):
        rows = buf[pl.ds(at + i * step, step), lanes_at : lanes_at + core, :]
        return rows.reshape(step * core, nm)

    return take


def add_gram(dst, a, b, first, last):
    def chunk(i, _):
        dst[...] += mm_t(a(i), b(i))
        return 0

    lax.fori_loop(first, last, chunk, 0)


def half_operator(x, weight, tmp, first, last, tall, core):
    nm = x.shape[2]
    c0, c1 = 2 * DEPTH, 2 * DEPTH + core

    def half(i, _):
        r = DEPTH + i
        ctr = x[r, c0:c1, :]
        spot = lax.broadcasted_iota(jnp.int32, (core, nm), 0)
        right = jnp.where(spot == core - 1, 0.0, x[r, c0 + 1 : c1 + 1, :])
        down = x[r + 1, c0:c1, :]
        down = jnp.where(i == tall - 1, jnp.zeros_like(down), down)
        tmp[i] = 0.25 * weight[r, c0:c1, :] * ctr + 0.2 * (right + down)
        return 0

    lax.fori_loop(first, last, half, 0)


def near_kernel(dims, pos, *refs):
    rows_here, group, wide, core = dims
    tall = rows_here * group
    known = tall + DEPTH
    n_near = group + group // 2
    at = 2 * group
    messages, refs = refs[:n_near], refs[n_near:]
    x, y, weight, start, gram1, gram2, ray, coup, cs, tmp = refs
    nm = x.shape[2]
    span = wide + 2 * DEPTH
    sign, col = pos[at], pl.multiple_of(pos[at + 1], 8)
    low, sides = pos[at + 2], (pos[at + 4], pos[at + 5])
    zero = jnp.zeros((2 * DEPTH, nm), jnp.float32)

    def clear(r, _):
        for buf in (x, y, weight):
            buf[r, 0 : 2 * DEPTH, :] = zero
            buf[r, span - 2 * DEPTH : span, :] = zero
        return 0

    lax.fori_loop(0, tall + 2 * DEPTH, clear, 0)
    blank = jnp.zeros((span, nm), jnp.float32)
    y[DEPTH - 1] = blank
    y[known] = blank
    spread(messages, (rows_here, wide), pos, col, 0, sign, x, weight, cs)
    for i in range(tall):
        start[i] = x[DEPTH + i, 2 * DEPTH : 2 * DEPTH + core, :]
    for total in (gram1, gram2, ray, coup):
        total[...] = jnp.zeros_like(total)
    take = block_rows(x, DEPTH, rows_here, 2 * DEPTH, core)
    for k in range(1, DEPTH + 1):
        dst, src = (y, x) if k % 2 else (x, y)
        apply_rows(
            dst, src, weight, wide, sides, jnp.maximum(low, k), known - k, k % DEGREE == 1
        )
        if k == DEGREE:
            add_gram(gram1, take, take, 0, group - DEGREE // rows_here)
    done = group // 2
    add_gram(gram2, take, take, 0, done)
    half_operator(x, weight, tmp, 0, (done - 1) * rows_here, tall, core)
    add_gram(ray, take, block_rows(tmp, 0, rows_here, 0, core), 0, done - 1)

    @pl.when(pos[at + 6] == 1)
    def _():
        add_gram(coup, block_rows(start, 0, rows_here, 0, core), take, 0, done)


def far_kernel(dims, pos, *refs):
    rows_here, group, wide, core = dims
    tall = rows_here * group
    known = tall + DEPTH
    n_far = group // 2
    at = 2 * group
    messages, refs = refs[:n_far], refs[n_far:]
    start, gram1_in, gram2_in, ray_in, coup_in, refs = *refs[3:8], refs[8:]
    x, y, weight, gram1, gram2, ray, coup, out, cs, tmp = refs
    sign, col = pos[at], pl.multiple_of(pos[at + 1], 8)
    high, sides = pos[at + 3], (pos[at + 4], pos[at + 5])
    spread(messages, (rows_here, wide), pos, col, group + group // 2, sign, x, weight, cs)
    for total, before in ((gram1, gram1_in), (gram2, gram2_in), (ray, ray_in), (coup, coup_in)):
        total[...] = before[...]
    take = block_rows(x, DEPTH, rows_here, 2 * DEPTH, core)
    for k in range(1, DEPTH + 1):
        dst, src = (y, x) if k % 2 else (x, y)
        apply_rows(
            dst,
            src,
            weight,
            wide,
            sides,
            known - k,
            jnp.minimum(high, known + DEPTH - k),
            k % DEGREE == 1,
        )
        if k == DEGREE:
            add_gram(gram1, take, take, group - DEGREE // rows_here, group)
    done = group // 2
    for i in range(tall):
        out[i] = x[DEPTH + i, 2 * DEPTH : 2 * DEPTH + core, :]
    add_gram(gram2, take, take, done, group)
    half_operator(x, weight, tmp, (done - 1) * rows_here, tall, tall, core)
    add_gram(ray, take, block_rows(tmp, 0, rows_here, 0, core), done - 1, group)

    @pl.when(pos[at + 6] == 1)
    def _():
        add_gram(coup, block_rows(start, 0, rows_here, 0, core), take, done, group)


def late_kernel(dims, turn, out, recv, down, right, ray0, coup0, ray, coup, side):
    rows_here, tall, core = dims
    coup[...] = coup0[...]
    add_gram(
        coup,
        block_rows(recv, 0, rows_here, 0, core),
        block_rows(out, 0, rows_here, 0, core),
        0,
        tall // rows_here,
    )
    for i in range(tall):
        side[i : i + 1, :] = right[turn[0] + turn[1] * i]
    ray[...] = ray0[...] + 0.2 * (
        mm_t(out[tall - 1], down[0]) + mm_t(out[:, core - 1, :], side[...])
    )


def modes_kernel(dims, pos, *refs):
    rows_here, group, core = dims
    blocks, mix, modes = refs[:group], refs[group], refs[group + 1]
    m = mix[...]
    for k in range(group):
        at = pl.multiple_of(pos[3 * k] * core, core)
        for r in range(rows_here):
            row = pos[3 * k + 1] + pos[3 * k + 2] * r
            modes[r, pl.ds(at, core), :] = mm(blocks[k][row], m)


SUB = 8

def inverse_factor(a, work, panel, w, big=32):
    n = a.shape[0]
    row_id = lax.broadcasted_iota(jnp.int32, (n, n), 0)
    col_id = lax.broadcasted_iota(jnp.int32, (n, n), 1)
    work[:, :n] = a
    work[:, n:] = (row_id == col_id).astype(jnp.float32)
    sub_id = lax.broadcasted_iota(jnp.int32, (SUB, n), 0)
    full = (SUB, n)
    for top in range(0, n, big):
        blocks = [
            [work[at : at + SUB, :n], work[at : at + SUB, n:]]
            for at in range(top, top + big, SUB)
        ]
        for j in range(big // SUB):
            at = top + j * SUB
            diag = blocks[j][0]
            e = {
                (i, k): jnp.broadcast_to(diag[i : i + 1, at + k : at + k + 1], full)
                for i in range(SUB)
                for k in range(i + 1)
            }
            low, inv = {}, []
            for k in range(SUB):
                inv.append(lax.rsqrt(e[k, k]))
                for i in range(k + 1, SUB):
                    low[i, k] = e[i, k] * inv[k]
                for m in range(k + 1, SUB):
                    for i in range(m, SUB):
                        e[i, m] = e[i, m] - low[i, k] * low[m, k]
            ups = []
            for k in range(SUB):
                row = [jnp.broadcast_to(part[k : k + 1, :], full) for part in blocks[j]]
                for m in range(k):
                    row = [p - low[k, m] * q for p, q in zip(row, ups[m])]
                ups.append([p * inv[k] for p in row])
            done = [ups[0][0], ups[0][1]]
            for k in range(1, SUB):
                done = [jnp.where(sub_id == k, p, q) for p, q in zip(ups[k], done)]
            blocks[j] = done
            for i in range(j + 1, big // SUB):
                cols = []
                for k in range(SUB):
                    c = jnp.broadcast_to(blocks[i][0][:, at + k : at + k + 1], full)
                    for m in range(k):
                        c = c - low[k, m] * cols[m]
                    cols.append(c * inv[k])
                for part in range(2):
                    for k in range(SUB):
                        blocks[i][part] = blocks[i][part] - cols[k] * ups[k][part]
        for j in range(big // SUB):
            at = top + j * SUB
            w[at : at + SUB, :] = blocks[j][1]
            panel[j * SUB : (j + 1) * SUB, :n] = blocks[j][0]
            panel[j * SUB : (j + 1) * SUB, n:] = blocks[j][1]
        if top + big < n:
            fix = mm_t(panel[:, :n], panel[...])
            work[top + big :, :] = work[top + big :, :] - fix[top + big :, :]

def mixing_kernel(scale, g1, g2, rot, order, mix, work, panel, w):
    n = g1.shape[0]
    ids = lax.broadcasted_iota(jnp.int32, (n, n), 0)
    def turned(t):
        pick = (order[t : t + 1, :] == ids).astype(jnp.float32)
        return mm(rot[t], pick)
    r1 = turned(0)
    inverse_factor(g1[...] * scale, work, panel, w)
    m1 = mm_t(w[...], r1)
    inverse_factor(mm_t(m1, mm(g2[...] * scale, m1)), work, panel, w)
    m2 = mm_t(w[...], turned(1))
    mix[...] = mm(m1, m2)


def xor_swap(value, axis, bit):
    peers = lax.axis_size(axis)
    return lax.ppermute(value, axis, [(i, i ^ bit) for i in range(peers)])


def sum_pair(one, two, axis):
    peers = lax.axis_size(axis)
    odd = (lax.axis_index(axis) & 1) == 1
    mine = jnp.where(odd, two, one) + xor_swap(jnp.where(odd, one, two), axis, 1)
    bit = 2
    while bit < peers:
        mine = mine + xor_swap(mine, axis, bit)
        bit *= 2
    other = xor_swap(mine, axis, 1)
    return jnp.where(odd, other, mine), jnp.where(odd, mine, other)


def body(start_modes, contrast, rotations, ordering):
    v0, section = start_modes[0], contrast[0]
    rows_here, columns, nm = v0.shape
    peers = lax.axis_size("rows")
    cuts = lax.axis_size("cuts")
    near = DEPTH // rows_here
    group = 2 * near
    core = columns // group
    wide = core + 2 * DEPTH
    tall = group * rows_here
    pixels = rows_here * peers * columns
    me = lax.axis_index("rows")
    cut = lax.axis_index("cuts")
    q = me % group
    block = me // group
    blocks = peers // group

    def window(k):
        at = jnp.clip((q ^ k) * core - DEPTH, 0, columns - wide)
        part = lax.dynamic_slice(v0, (0, at, 0), (rows_here, wide, nm)).reshape(-1, nm)
        tail = lax.dynamic_slice(section, (0, at), (rows_here, wide))
        tail = jnp.pad(tail, ((0, 0), (0, 2 * LANES - wide))).reshape(2 * rows_here, LANES)
        return jnp.concatenate([part, tail], axis=0)

    def hop(j, relayed=False):
        pairs = []
        for i in range(peers):
            z, s = i // group, i % group
            to = z + 1 if (s >= near) != relayed else z - 1
            if 0 <= to < blocks:
                pairs.append((i, to * group + (s ^ j)))
        return pairs

    windows = [window(k) for k in range(group)]
    arrived = [None] * group
    for k in reversed(range(1, group)):
        arrived[k] = xor_swap(windows[k], "rows", k)
    direct = [lax.ppermute(windows[j], "rows", hop(j)) for j in range(near)]
    relay = [lax.ppermute(arrived[k], "rows", hop(0, True)) for k in range(near, group)]
    messages = [windows[0]] + arrived[1:] + direct + relay

    lower = q >= near
    total = tall + 2 * DEPTH
    sign = jnp.where(lower, 1, -1)
    image = [DEPTH + (q ^ k) * rows_here for k in range(group)]
    for j in range(near):
        s = q ^ j
        image.append(jnp.where(lower, (s - near) * rows_here, DEPTH + tall + s * rows_here))
    for k in range(near, group):
        s = q ^ k
        image.append(jnp.where(lower, DEPTH + tall + s * rows_here, (s - near) * rows_here))
    at = jnp.clip(q * core - DEPTH, 0, columns - wide)
    top, bottom = block == 0, block == blocks - 1
    no_near = jnp.where(lower, top, bottom)
    no_far = jnp.where(lower, bottom, top)
    place = [jnp.where(lower, i, total - 1 - i) for i in image] + [
        sign,
        DEPTH + at - (q * core - DEPTH),
        jnp.where(no_near, DEPTH, 0),
        jnp.where(no_far, DEPTH + tall, total),
        q == 0,
        q == group - 1,
        cut == 0,
    ]
    place = jnp.stack([jnp.asarray(p, jnp.int32) for p in place])

    square = jax.ShapeDtypeStruct((nm, nm), jnp.float32)
    tile = jax.ShapeDtypeStruct((tall, core, nm), jnp.float32)
    span = wide + 2 * DEPTH
    field_buffer = jax.ShapeDtypeStruct((total, span, nm), jnp.float32)
    vmem = pl.BlockSpec(memory_space=pltpu.VMEM)
    smem = pl.BlockSpec(memory_space=pltpu.SMEM)
    params = pltpu.CompilerParams(vmem_limit_bytes=16 * 1024 * 1024)
    dims = (rows_here, group, wide, core)
    early, far = messages[: group + near], messages[group + near :]
    x, y, weight, start, *sums = pl.pallas_call(
        functools.partial(near_kernel, dims),
        out_shape=(field_buffer,) * 3 + (tile,) + (square,) * 4,
        in_specs=[smem] + [vmem] * len(early),
        out_specs=[vmem] * 8,
        scratch_shapes=[
            pltpu.VMEM((2 * rows_here * len(early), LANES), jnp.float32),
            pltpu.VMEM((tall, core, nm), jnp.float32),
        ],
        compiler_params=params,
        cost_estimate=pl.CostEstimate(flops=10**9, bytes_accessed=4 * 10**7, transcendentals=0),
        name="near",
    )(place, *early)
    n_far = len(far)
    *_, gram1, gram2, ray, coup, field = pl.pallas_call(
        functools.partial(far_kernel, dims),
        out_shape=(field_buffer,) * 3 + (square,) * 4 + (tile,),
        in_specs=[smem] + [vmem] * (n_far + 8),
        out_specs=[vmem] * 8,
        input_output_aliases={1 + n_far + i: i for i in range(3)},
        scratch_shapes=[
            pltpu.VMEM((2 * rows_here * n_far, LANES), jnp.float32),
            pltpu.VMEM((tall, core, nm), jnp.float32),
        ],
        compiler_params=params,
        cost_estimate=pl.CostEstimate(flops=10**9, bytes_accessed=2 * 10**7, transcendentals=0),
        name="far",
    )(place, *far, x, y, weight, start, *sums)

    recv = lax.ppermute(field, "cuts", [(i, i + 1) for i in range(cuts - 1)])
    down = lax.ppermute(field[:1], "rows", hop(0, True))
    right = lax.ppermute(
        field[:, :1], "rows", [(i + 1, i) for i in range(peers) if i % group != group - 1]
    )
    back = []
    for k in range(1, group):
        s = (q ^ k) * rows_here
        part = lax.dynamic_slice_in_dim(
            field, jnp.where(lower, s, tall - rows_here - s), rows_here, 0
        )
        back.append(xor_swap(part, "rows", k))

    gram1, gram2 = sum_pair(gram1, gram2, "rows")
    big = min(nm, 32)
    mix = pl.pallas_call(
        functools.partial(mixing_kernel, 1.0 / pixels),
        out_shape=square,
        in_specs=[vmem] * 4,
        out_specs=vmem,
        compiler_params=params,
        cost_estimate=pl.CostEstimate(flops=10**9, bytes_accessed=4 * 10**7, transcendentals=0),
        scratch_shapes=[
            pltpu.VMEM((nm, 2 * nm), jnp.float32),
            pltpu.VMEM((big, 2 * nm), jnp.float32),
            pltpu.VMEM((nm, nm), jnp.float32),
        ],
        name="mixing",
    )(gram1, gram2, rotations[0], ordering[0])

    turned = q == near - 1
    turn = jnp.stack([jnp.where(turned, tall - 1, 0), jnp.where(turned, -1, 1)])
    ray, coup = pl.pallas_call(
        functools.partial(late_kernel, (rows_here, tall, core)),
        out_shape=(square, square),
        in_specs=[smem] + [vmem] * 6,
        out_specs=[vmem] * 2,
        scratch_shapes=[pltpu.VMEM((tall, nm), jnp.float32)],
        compiler_params=params,
        cost_estimate=pl.CostEstimate(flops=10**9, bytes_accessed=10**7, transcendentals=0),
        name="late",
    )(turn.astype(jnp.int32), field, recv, down, right, ray, coup)
    ray, coup = sum_pair(ray, coup, "rows")

    before = lax.ppermute(mix, "cuts", [(i, i + 1) for i in range(cuts - 1)])
    eye = (jnp.arange(nm)[:, None] == jnp.arange(nm)[None, :]).astype(jnp.float32)
    before = jnp.where(cut == 0, eye, before)
    share = nm // peers
    mine = me * share
    left = lax.dynamic_slice_in_dim(before, mine, share, 1)
    coupling = mm(mm(left.T, coup), mix) / pixels
    left = lax.dynamic_slice_in_dim(mix, mine, share, 1)
    rayleigh = mm(mm(left.T, ray + ray.T), mix) / pixels

    where = []
    for k in range(group):
        source = q ^ k
        base = 0
        if k == 0:
            base = jnp.where(lower, q * rows_here, tall - rows_here - q * rows_here)
        down_there = source >= near
        where += [
            source,
            jnp.where(down_there, base, base + rows_here - 1),
            jnp.where(down_there, 1, -1),
        ]
    where = jnp.stack([jnp.asarray(p, jnp.int32) for p in where])
    modes = pl.pallas_call(
        functools.partial(modes_kernel, (rows_here, group, core)),
        out_shape=jax.ShapeDtypeStruct((rows_here, columns, nm), jnp.float32),
        in_specs=[smem] + [vmem] * (group + 1),
        out_specs=vmem,
        compiler_params=params,
        cost_estimate=pl.CostEstimate(flops=10**9, bytes_accessed=10**7, transcendentals=0),
        name="modes",
    )(where, field, *back, mix)
    return modes[None], coupling[None], rayleigh[None]


def solution(mesh):
    placed = (
        P("cuts", "rows", None, None),
        P("cuts", "rows", None),
        P("cuts", None, None, None),
        P("cuts", None, None),
    )
    return jax.shard_map(
        body,
        mesh=mesh,
        in_specs=placed,
        out_specs=(P("cuts", "rows", None, None), P("cuts", "rows", None), P("cuts", "rows", None)),
        check_vma=False,
    )
```

```python
import functools

import jax
import jax.numpy as jnp
from jax import lax
from jax.experimental import pallas as pl
from jax.experimental.pallas import tpu as pltpu
from jax.sharding import PartitionSpec as P


DEGREE = 4
ITERS = 2
DEPTH = DEGREE * ITERS
LANES = 128
HIGHEST = lax.Precision.HIGHEST


def mm(a, b):
    return jnp.dot(a, b, precision=HIGHEST, preferred_element_type=jnp.float32)


def mm_t(a, b):
    return lax.dot_general(
        a, b, (((0,), (0,)), ((), ())), precision=HIGHEST, preferred_element_type=jnp.float32
    )


def spread(messages, dims, pos, col, at, sign, x, weight, cs):
    rows_here, wide = dims
    nm = x.shape[2]
    for i, message in enumerate(messages):
        for r in range(rows_here):
            x[pos[at + i] + sign * r, pl.ds(col, wide), :] = message[r * wide : (r + 1) * wide, :]
        cs[2 * rows_here * i : 2 * rows_here * (i + 1), :] = message[rows_here * wide :, :]
    turned = (1.6 * cs[...] - 0.4).T
    for i in range(len(messages)):
        for r in range(rows_here):
            row = pos[at + i] + sign * r
            c = 2 * (rows_here * i + r)
            weight[row, pl.ds(col, LANES), :] = jnp.broadcast_to(
                turned[:, c : c + 1], (LANES, nm)
            )
            weight[row, pl.ds(pl.multiple_of(col + LANES, 8), wide - LANES), :] = (
                jnp.broadcast_to(turned[: wide - LANES, c + 1 : c + 2], (wide - LANES, nm))
            )


def apply_rows(dst, src, weight, wide, sides, first, last, opening):
    left = DEPTH
    at_left, at_right = sides
    count = last - first
    strip = wide // 3 if wide % 24 == 0 else wide
    unroll = 4

    for c0 in range(left, left + wide, strip):
        c1 = c0 + strip

        def row(r, up, ctr, c0=c0, c1=c1):
            down = src[r + 1, c0:c1, :]
            s = (up + down) + (src[r, c0 - 1 : c1 - 1, :] + src[r, c0 + 1 : c1 + 1, :])
            v = weight[r, c0:c1, :] * ctr + 0.4 * s
            if opening:
                v = 0.5 * v
            else:
                v = v - dst[r, c0:c1, :]
            a, b = c0, c1
            if c0 == left:
                edge = v[:DEPTH]
                dst[r, a : a + DEPTH, :] = jnp.where(at_left == 1, jnp.zeros_like(edge), edge)
                v, a = v[DEPTH:], a + DEPTH
            if c1 == left + wide:
                edge = v[b - DEPTH - a :]
                dst[r, b - DEPTH : b, :] = jnp.where(at_right == 1, jnp.zeros_like(edge), edge)
                v, b = v[: b - DEPTH - a], b - DEPTH
            dst[r, a:b, :] = v
            return ctr, down

        def rows(i, pair):
            for j in range(unroll):
                pair = row(first + unroll * i + j, *pair)
            return pair

        pair = (src[first - 1, c0:c1, :], src[first, c0:c1, :])
        whole = count // unroll
        if whole > 1:
            pair = lax.fori_loop(0, whole, rows, pair)
        elif whole:
            pair = rows(0, pair)
        for r in range(first + whole * unroll, last):
            pair = row(r, *pair)


def halves(v):
    high = v.astype(jnp.bfloat16)
    low = (v - high.astype(jnp.float32)).astype(jnp.bfloat16)
    return jnp.concatenate([high, low], axis=1)


def fold(p):
    n, m = p.shape[0] // 2, p.shape[1] // 2
    return (p[:n, :m] + p[n:, m:]) + (p[:n, m:] + p[n:, :m])


def block_rows(buf, at, step, lanes_at, core):
    nm = buf.shape[2]

    def take(first, last):
        rows = buf[at + first * step : at + last * step, lanes_at : lanes_at + core, :]
        return halves(rows.reshape((last - first) * step * core, nm))

    return take


def add_gram(dst, a, b, first, last):
    left = a(first, last)
    right = left if b is a else b(first, last)
    dst[...] += fold(
        lax.dot_general(
            left, right, (((0,), (0,)), ((), ())), preferred_element_type=jnp.float32
        )
    )


def half_operator(x, weight, tmp, first, last, tall, core):
    nm = x.shape[2]
    c0, c1 = 2 * DEPTH, 2 * DEPTH + core

    def half(i, _):
        r = DEPTH + i
        ctr = x[r, c0:c1, :]
        spot = lax.broadcasted_iota(jnp.int32, (core, nm), 0)
        right = jnp.where(spot == core - 1, 0.0, x[r, c0 + 1 : c1 + 1, :])
        down = x[r + 1, c0:c1, :]
        down = jnp.where(i == tall - 1, jnp.zeros_like(down), down)
        tmp[i] = 0.25 * weight[r, c0:c1, :] * ctr + 0.2 * (right + down)
        return 0

    lax.fori_loop(first, last, half, 0)


def near_kernel(dims, pos, *refs):
    rows_here, group, wide, core = dims
    tall = rows_here * group
    known = tall + DEPTH
    n_near = group + group // 2
    at = 2 * group
    messages, refs = refs[:n_near], refs[n_near:]
    x, y, weight, start, gram1, gram2, ray, coup, cs, tmp = refs
    nm = x.shape[2]
    span = wide + 2 * DEPTH
    sign, col = pos[at], pl.multiple_of(pos[at + 1], 8)
    low, sides = pos[at + 2], (pos[at + 4], pos[at + 5])
    zero = jnp.zeros((2 * DEPTH, nm), jnp.float32)

    def clear(r, _):
        for buf in (x, y, weight):
            buf[r, 0 : 2 * DEPTH, :] = zero
            buf[r, span - 2 * DEPTH : span, :] = zero
        return 0

    lax.fori_loop(0, tall + 2 * DEPTH, clear, 0)
    blank = jnp.zeros((span, nm), jnp.float32)
    y[DEPTH - 1] = blank
    y[known] = blank
    spread(messages, (rows_here, wide), pos, col, 0, sign, x, weight, cs)
    for i in range(tall):
        start[i] = x[DEPTH + i, 2 * DEPTH : 2 * DEPTH + core, :]
    for total in (gram1, gram2, ray, coup):
        total[...] = jnp.zeros_like(total)
    take = block_rows(x, DEPTH, rows_here, 2 * DEPTH, core)
    for k in range(1, DEPTH + 1):
        dst, src = (y, x) if k % 2 else (x, y)
        opening = k % DEGREE == 1
        if k < DEPTH:

            @pl.when(low < DEPTH)
            def _(dst=dst, src=src, k=k, opening=opening):
                apply_rows(dst, src, weight, wide, sides, k, DEPTH, opening)

        apply_rows(dst, src, weight, wide, sides, DEPTH, known - k, opening)
        if k == DEGREE:
            add_gram(gram1, take, take, 0, group - DEGREE // rows_here)
    done = group // 2
    add_gram(gram2, take, take, 0, done)
    half_operator(x, weight, tmp, 0, (done - 1) * rows_here, tall, core)
    add_gram(ray, take, block_rows(tmp, 0, rows_here, 0, core), 0, done - 1)

    @pl.when(pos[at + 6] == 1)
    def _():
        add_gram(coup, take, block_rows(start, 0, rows_here, 0, core), 0, done)


def far_kernel(dims, pos, *refs):
    rows_here, group, wide, core = dims
    tall = rows_here * group
    known = tall + DEPTH
    n_far = group // 2
    at = 2 * group
    messages, refs = refs[:n_far], refs[n_far:]
    start, gram1_in, gram2_in, ray_in, coup_in, refs = *refs[3:8], refs[8:]
    x, y, weight, gram1, gram2, ray, coup, out, row0 = refs[:9]
    backs, cs, tmp = refs[9 : 8 + group], refs[8 + group], refs[9 + group]
    sign, col = pos[at], pl.multiple_of(pos[at + 1], 8)
    high, sides = pos[at + 3], (pos[at + 4], pos[at + 5])
    spread(messages, (rows_here, wide), pos, col, group + group // 2, sign, x, weight, cs)
    for total, before in ((gram1, gram1_in), (gram2, gram2_in), (ray, ray_in), (coup, coup_in)):
        total[...] = before[...]
    take = block_rows(x, DEPTH, rows_here, 2 * DEPTH, core)
    for k in range(1, DEPTH + 1):
        dst, src = (y, x) if k % 2 else (x, y)
        opening = k % DEGREE == 1
        apply_rows(dst, src, weight, wide, sides, known - k, known, opening)
        if k < DEPTH:

            @pl.when(high > known)
            def _(dst=dst, src=src, k=k, opening=opening):
                apply_rows(dst, src, weight, wide, sides, known, known + DEPTH - k, opening)

        if k == DEGREE:
            add_gram(gram1, take, take, group - DEGREE // rows_here, group)
    done = group // 2
    for i in range(tall):
        out[i] = x[DEPTH + i, 2 * DEPTH : 2 * DEPTH + core, :]
        for back in backs:
            at_end = rows_here * core + i
            back[at_end : at_end + 1, :] = x[DEPTH + i, 2 * DEPTH : 2 * DEPTH + 1, :]
    row0[...] = x[DEPTH, 2 * DEPTH : 2 * DEPTH + core, :]
    for k, back in enumerate(backs):
        for r in range(rows_here):
            back[r * core : (r + 1) * core, :] = x[
                DEPTH + pos[at + 7 + k] + r, 2 * DEPTH : 2 * DEPTH + core, :
            ]
    add_gram(gram2, take, take, done, group)
    half_operator(x, weight, tmp, (done - 1) * rows_here, tall, tall, core)
    add_gram(ray, take, block_rows(tmp, 0, rows_here, 0, core), done - 1, group)

    @pl.when(pos[at + 6] == 1)
    def _():
        add_gram(coup, take, block_rows(start, 0, rows_here, 0, core), done, group)


def late_kernel(dims, turn, out, recv, down, ray0, coup0, *refs):
    rows_here, tall, core = dims
    columns, (ray, coup, side) = refs[:-3], refs[-3:]
    coup[...] = coup0[...]
    add_gram(
        coup,
        block_rows(out, 0, rows_here, 0, core),
        block_rows(recv, 0, rows_here, 0, core),
        0,
        tall // rows_here,
    )
    for i in range(tall):
        total = jnp.zeros((1, side.shape[1]), jnp.float32)
        for k, column in enumerate(columns):
            there = column[pl.ds(rows_here * core + turn[0] + turn[1] * i, 1), :]
            total = jnp.where(turn[2 + k] == 1, there, total)
        side[i : i + 1, :] = total
    ray[...] = ray0[...] + 0.2 * (
        mm_t(out[tall - 1], down[...]) + mm_t(out[:, core - 1, :], side[...])
    )


def modes_kernel(dims, pos, *refs):
    rows_here, group, core = dims
    blocks, mix, modes = refs[:group], refs[group], refs[group + 1]
    nm = mix.shape[0]
    m = halves(mix[...])
    m = jnp.concatenate([m, m], axis=0)
    for k in range(group):
        at = pl.multiple_of(pos[3 * k] * core, core)
        for r in range(rows_here):
            row = pos[3 * k + 1] + pos[3 * k + 2] * r
            if k:
                v = blocks[k][pl.ds(pl.multiple_of(row * core, core), core), :]
            else:
                v = blocks[k][row]
            p = jnp.dot(halves(v), m, preferred_element_type=jnp.float32)
            modes[r, pl.ds(at, core), :] = p[:, :nm] + p[:, nm:]


SUB = 8


def inverse_factor(a, work, panel, w, big=32):
    n = a.shape[0]
    row_id = lax.broadcasted_iota(jnp.int32, (n, n), 0)
    col_id = lax.broadcasted_iota(jnp.int32, (n, n), 1)
    work[:, :n] = a
    work[:, n:] = (row_id == col_id).astype(jnp.float32)
    sub_id = lax.broadcasted_iota(jnp.int32, (SUB, n), 0)
    full = (SUB, n)
    for top in range(0, n, big):
        blocks = [
            [work[at : at + SUB, :n], work[at : at + SUB, n:]]
            for at in range(top, top + big, SUB)
        ]
        for j in range(big // SUB):
            at = top + j * SUB
            diag = blocks[j][0]
            e = {
                (i, k): jnp.broadcast_to(diag[i : i + 1, at + k : at + k + 1], full)
                for i in range(SUB)
                for k in range(i + 1)
            }
            low, inv = {}, []
            for k in range(SUB):
                inv.append(lax.rsqrt(e[k, k]))
                for i in range(k + 1, SUB):
                    low[i, k] = e[i, k] * inv[k]
                for m in range(k + 1, SUB):
                    for i in range(m, SUB):
                        e[i, m] = e[i, m] - low[i, k] * low[m, k]
            ups = []
            for k in range(SUB):
                row = [jnp.broadcast_to(part[k : k + 1, :], full) for part in blocks[j]]
                for m in range(k):
                    row = [p - low[k, m] * q for p, q in zip(row, ups[m])]
                ups.append([p * inv[k] for p in row])
            done = [ups[0][0], ups[0][1]]
            for k in range(1, SUB):
                done = [jnp.where(sub_id == k, p, q) for p, q in zip(ups[k], done)]
            blocks[j] = done
            for i in range(j + 1, big // SUB):
                cols = []
                for k in range(SUB):
                    c = jnp.broadcast_to(blocks[i][0][:, at + k : at + k + 1], full)
                    for m in range(k):
                        c = c - low[k, m] * cols[m]
                    cols.append(c * inv[k])
                for part in range(2):
                    for k in range(SUB):
                        blocks[i][part] = blocks[i][part] - cols[k] * ups[k][part]
        for j in range(big // SUB):
            at = top + j * SUB
            w[at : at + SUB, :] = blocks[j][1]
            panel[j * SUB : (j + 1) * SUB, :n] = blocks[j][0]
            panel[j * SUB : (j + 1) * SUB, n:] = blocks[j][1]
        if top + big < n:
            fix = mm_t(panel[:, :n], panel[...])
            work[top + big :, :] = work[top + big :, :] - fix[top + big :, :]


def mixing_kernel(scale, g1, g2, rot_at, order, mix, work, panel, w, rot, sem):
    fetch = pltpu.make_async_copy(rot_at, rot, sem)
    fetch.start()
    n = g1.shape[0]
    ids = lax.broadcasted_iota(jnp.int32, (n, n), 0)

    def turned(t):
        pick = (order[t : t + 1, :] == ids).astype(jnp.float32)
        return mm(rot[t], pick)

    inverse_factor(g1[...] * scale, work, panel, w)
    fetch.wait()
    m1 = mm_t(w[...], turned(0))
    inverse_factor(mm_t(m1, mm(g2[...] * scale, m1)), work, panel, w)
    m2 = mm_t(w[...], turned(1))
    mix[...] = mm(m1, m2)


def reversed_bits(value, count):
    out = 0
    while count > 1:
        out, value, count = 2 * out + value % 2, value // 2, count // 2
    return out


def project_kernel(peers, scale, first, ray, coup, before, mix, shares):
    nm = mix.shape[0]
    share = nm // peers
    m = mix[...] * scale

    def place(value, at):
        for r in range(peers):
            to = (2 * reversed_bits(r, peers) + at) * share
            shares[to : to + share, :] = value[r * share : (r + 1) * share, :]

    place(mm_t(mix[...], mm(ray[...] + ray[...].T, m)), 1)
    half = mm_t(coup[...], m)

    @pl.when(first[0] == 1)
    def _():
        place(half, 0)

    @pl.when(first[0] != 1)
    def _():
        place(mm_t(before[...], half), 0)


def scatter_sum(value, axis):
    peers = lax.axis_size(axis)
    me = lax.axis_index(axis)
    bit = 1
    while bit < peers:
        half = value.shape[0] // 2
        odd = (me & bit) != 0
        low, high = value[:half], value[half:]
        other = xor_swap(jnp.where(odd, low, high), axis, bit)
        value = jnp.where(odd, high, low) + other
        bit *= 2
    return value


def xor_swap(value, axis, bit):
    peers = lax.axis_size(axis)
    return lax.ppermute(value, axis, [(i, i ^ bit) for i in range(peers)])


def sum_pair(one, two, axis):
    peers = lax.axis_size(axis)
    odd = (lax.axis_index(axis) & 1) == 1
    mine, other, bit = jnp.where(odd, two, one), jnp.where(odd, one, two), 1
    while bit < peers:
        there = xor_swap(other, axis, bit)
        mine = mine + there
        other, bit = mine, 2 * bit
    other = xor_swap(mine, axis, 1)
    return jnp.where(odd, other, mine), jnp.where(odd, mine, other)


def body(start_modes, contrast, rotations, ordering):
    v0, section = start_modes[0], contrast[0]
    rows_here, columns, nm = v0.shape
    peers = lax.axis_size("rows")
    cuts = lax.axis_size("cuts")
    near = DEPTH // rows_here
    group = 2 * near
    core = columns // group
    wide = core + 2 * DEPTH
    tall = group * rows_here
    pixels = rows_here * peers * columns
    me = lax.axis_index("rows")
    cut = lax.axis_index("cuts")
    q = me % group
    block = me // group
    blocks = peers // group

    def window(k):
        at = jnp.clip((q ^ k) * core - DEPTH, 0, columns - wide)
        part = lax.dynamic_slice(v0, (0, at, 0), (rows_here, wide, nm)).reshape(-1, nm)
        tail = lax.dynamic_slice(section, (0, at), (rows_here, wide))
        tail = jnp.pad(tail, ((0, 0), (0, 2 * LANES - wide))).reshape(2 * rows_here, LANES)
        return jnp.concatenate([part, tail], axis=0)

    def hop(j, relayed=False):
        pairs = []
        for i in range(peers):
            z, s = i // group, i % group
            to = z + 1 if (s >= near) != relayed else z - 1
            if 0 <= to < blocks:
                pairs.append((i, to * group + (s ^ j)))
        return pairs

    windows = [window(k) for k in range(group)]
    arrived = [None] * group
    for k in reversed(range(1, group)):
        arrived[k] = xor_swap(windows[k], "rows", k)
    direct = [lax.ppermute(windows[j], "rows", hop(j)) for j in range(near)]
    relay = [lax.ppermute(arrived[k], "rows", hop(0, True)) for k in range(near, group)]
    messages = [windows[0]] + arrived[1:] + direct + relay

    lower = q >= near
    total = tall + 2 * DEPTH
    sign = jnp.where(lower, 1, -1)
    image = [DEPTH + (q ^ k) * rows_here for k in range(group)]
    for j in range(near):
        s = q ^ j
        image.append(jnp.where(lower, (s - near) * rows_here, DEPTH + tall + s * rows_here))
    for k in range(near, group):
        s = q ^ k
        image.append(jnp.where(lower, DEPTH + tall + s * rows_here, (s - near) * rows_here))
    at = jnp.clip(q * core - DEPTH, 0, columns - wide)
    top, bottom = block == 0, block == blocks - 1
    no_near = jnp.where(lower, top, bottom)
    no_far = jnp.where(lower, bottom, top)
    place = [jnp.where(lower, i, total - 1 - i) for i in image] + [
        sign,
        DEPTH + at - (q * core - DEPTH),
        jnp.where(no_near, DEPTH, 0),
        jnp.where(no_far, DEPTH + tall, total),
        q == 0,
        q == group - 1,
        cut == 0,
    ]
    for k in range(1, group):
        s = (q ^ k) * rows_here
        place.append(jnp.where(lower, s, tall - rows_here - s))
    place = jnp.stack([jnp.asarray(p, jnp.int32) for p in place])

    square = jax.ShapeDtypeStruct((nm, nm), jnp.float32)
    tile = jax.ShapeDtypeStruct((tall, core, nm), jnp.float32)
    span = wide + 2 * DEPTH
    field_buffer = jax.ShapeDtypeStruct((total, span, nm), jnp.float32)
    vmem = pl.BlockSpec(memory_space=pltpu.VMEM)
    smem = pl.BlockSpec(memory_space=pltpu.SMEM)
    params = pltpu.CompilerParams(vmem_limit_bytes=16 * 1024 * 1024)
    dims = (rows_here, group, wide, core)
    early, far = messages[: group + near], messages[group + near :]
    x, y, weight, start, *sums = pl.pallas_call(
        functools.partial(near_kernel, dims),
        out_shape=(field_buffer,) * 3 + (tile,) + (square,) * 4,
        in_specs=[smem] + [vmem] * len(early),
        out_specs=[vmem] * 8,
        scratch_shapes=[
            pltpu.VMEM((2 * rows_here * len(early), LANES), jnp.float32),
            pltpu.VMEM((tall, core, nm), jnp.float32),
        ],
        compiler_params=params,
        cost_estimate=pl.CostEstimate(flops=10**9, bytes_accessed=4 * 10**7, transcendentals=0),
        name="near",
    )(place, *early)
    n_far = len(far)
    back_block = jax.ShapeDtypeStruct((rows_here * core + tall, nm), jnp.float32)
    _, _, _, gram1, gram2, ray, coup, field, row0, *back = pl.pallas_call(
        functools.partial(far_kernel, dims),
        out_shape=(field_buffer,) * 3
        + (square,) * 4
        + (tile, jax.ShapeDtypeStruct((core, nm), jnp.float32))
        + (back_block,) * (group - 1),
        in_specs=[smem] + [vmem] * (n_far + 8),
        out_specs=[vmem] * (8 + group),
        input_output_aliases={1 + n_far + i: i for i in range(3)},
        scratch_shapes=[
            pltpu.VMEM((2 * rows_here * n_far, LANES), jnp.float32),
            pltpu.VMEM((tall, core, nm), jnp.float32),
        ],
        compiler_params=params,
        cost_estimate=pl.CostEstimate(flops=10**9, bytes_accessed=2 * 10**7, transcendentals=0),
        name="far",
    )(place, *far, x, y, weight, start, *sums)

    recv = lax.ppermute(field, "cuts", [(i, i + 1) for i in range(cuts - 1)])
    gram1, gram2 = sum_pair(gram1, gram2, "rows")
    down = lax.ppermute(row0, "rows", hop(0, True))
    sent = back
    back = []
    for k in range(1, group):
        back.append(xor_swap(sent[k - 1], "rows", k))

    big = min(nm, 32)
    mix = pl.pallas_call(
        functools.partial(mixing_kernel, 1.0 / pixels),
        out_shape=square,
        in_specs=[vmem, vmem, pl.BlockSpec(memory_space=pl.ANY), vmem],
        out_specs=vmem,
        compiler_params=params,
        cost_estimate=pl.CostEstimate(flops=10**9, bytes_accessed=4 * 10**7, transcendentals=0),
        scratch_shapes=[
            pltpu.VMEM((nm, 2 * nm), jnp.float32),
            pltpu.VMEM((big, 2 * nm), jnp.float32),
            pltpu.VMEM((nm, nm), jnp.float32),
            pltpu.VMEM(rotations.shape[1:], jnp.float32),
            pltpu.SemaphoreType.DMA,
        ],
        name="mixing",
    )(gram1, gram2, rotations[0], ordering[0])

    before = lax.ppermute(mix, "cuts", [(i, i + 1) for i in range(cuts - 1)])
    edges = [k for k in range(1, group) if k & (k + 1) == 0]
    beside = [back[k - 1] for k in edges]
    recv, down, beside, mix_now = lax.optimization_barrier((recv, down, beside, mix))
    turned = q == near - 1
    turn = [jnp.where(turned, tall - 1, 0), jnp.where(turned, -1, 1)]
    turn += [(((q ^ (q + 1)) == k) & (q != group - 1)).astype(jnp.int32) for k in edges]
    turn = jnp.stack(turn)
    ray, coup = pl.pallas_call(
        functools.partial(late_kernel, (rows_here, tall, core)),
        out_shape=(square, square),
        in_specs=[smem] + [vmem] * (5 + len(edges)),
        out_specs=[vmem] * 2,
        scratch_shapes=[pltpu.VMEM((tall, nm), jnp.float32)],
        compiler_params=params,
        cost_estimate=pl.CostEstimate(flops=10**9, bytes_accessed=10**7, transcendentals=0),
        name="late",
    )(turn.astype(jnp.int32), field, recv, down, ray, coup, *beside)
    share = nm // peers
    first = (cut == 0).astype(jnp.int32).reshape(1)
    shares = pl.pallas_call(
        functools.partial(project_kernel, peers, 1.0 / pixels),
        out_shape=jax.ShapeDtypeStruct((2 * nm, nm), jnp.float32),
        in_specs=[smem] + [vmem] * 4,
        out_specs=vmem,
        compiler_params=params,
        cost_estimate=pl.CostEstimate(flops=10**8, bytes_accessed=10**6, transcendentals=0),
        name="project",
    )(first, ray, coup, before, mix_now)
    shares = scatter_sum(shares, "rows")
    coupling, rayleigh = shares[:share], shares[share:]

    where = []
    for k in range(group):
        source = q ^ k
        base = 0
        if k == 0:
            base = jnp.where(lower, q * rows_here, tall - rows_here - q * rows_here)
        down_there = source >= near
        where += [
            source,
            jnp.where(down_there, base, base + rows_here - 1),
            jnp.where(down_there, 1, -1),
        ]
    where = jnp.stack([jnp.asarray(p, jnp.int32) for p in where])
    modes = pl.pallas_call(
        functools.partial(modes_kernel, (rows_here, group, core)),
        out_shape=jax.ShapeDtypeStruct((rows_here, columns, nm), jnp.float32),
        in_specs=[smem] + [vmem] * (group + 1),
        out_specs=vmem,
        compiler_params=params,
        cost_estimate=pl.CostEstimate(flops=10**9, bytes_accessed=10**7, transcendentals=0),
        name="modes",
    )(where, field, *back, mix)
    return modes[None], coupling[None], rayleigh[None]


def solution(mesh):
    placed = (
        P("cuts", "rows", None, None),
        P("cuts", "rows", None),
        P("cuts", None, None, None),
        P("cuts", None, None),
    )

    return jax.shard_map(
        body,
        mesh=mesh,
        in_specs=placed,
        out_specs=(P("cuts", "rows", None, None), P("cuts", "rows", None), P("cuts", "rows", None)),
        check_vma=False,
    )
```

```python
import functools

import jax
import jax.numpy as jnp
from jax import lax
from jax.experimental import pallas as pl
from jax.experimental.pallas import tpu as pltpu
from jax.sharding import PartitionSpec as P


DEGREE = 4
ITERS = 2
DEPTH = DEGREE * ITERS
LANES = 128
HIGHEST = lax.Precision.HIGHEST


def mm(a, b):
    return jnp.dot(a, b, precision=HIGHEST, preferred_element_type=jnp.float32)


def mm_t(a, b):
    return lax.dot_general(
        a, b, (((0,), (0,)), ((), ())), precision=HIGHEST, preferred_element_type=jnp.float32
    )


def spread(messages, dims, pos, col, at, sign, x, weight, cs):
    rows_here, wide = dims
    nm = x.shape[2]
    for i, message in enumerate(messages):
        for r in range(rows_here):
            x[pos[at + i] + sign * r, pl.ds(col, wide), :] = message[r * wide : (r + 1) * wide, :]
        cs[2 * rows_here * i : 2 * rows_here * (i + 1), :] = message[rows_here * wide :, :]
    turned = (1.6 * cs[...] - 0.4).T
    for i in range(len(messages)):
        for r in range(rows_here):
            row = pos[at + i] + sign * r
            c = 2 * (rows_here * i + r)
            weight[row, pl.ds(col, LANES), :] = jnp.broadcast_to(
                turned[:, c : c + 1], (LANES, nm)
            )
            weight[row, pl.ds(pl.multiple_of(col + LANES, 8), wide - LANES), :] = (
                jnp.broadcast_to(turned[: wide - LANES, c + 1 : c + 2], (wide - LANES, nm))
            )


def apply_rows(dst, src, weight, wide, sides, first, last, opening):
    left = DEPTH
    at_left, at_right = sides
    count = last - first
    strip = wide // 3 if wide % 24 == 0 else wide
    unroll = 4

    for c0 in range(left, left + wide, strip):
        c1 = c0 + strip

        def row(r, up, ctr, c0=c0, c1=c1):
            down = src[r + 1, c0:c1, :]
            s = (up + down) + (src[r, c0 - 1 : c1 - 1, :] + src[r, c0 + 1 : c1 + 1, :])
            v = weight[r, c0:c1, :] * ctr + 0.4 * s
            if opening:
                v = 0.5 * v
            else:
                v = v - dst[r, c0:c1, :]
            a, b = c0, c1
            if c0 == left:
                edge = v[:DEPTH]
                dst[r, a : a + DEPTH, :] = jnp.where(at_left == 1, jnp.zeros_like(edge), edge)
                v, a = v[DEPTH:], a + DEPTH
            if c1 == left + wide:
                edge = v[b - DEPTH - a :]
                dst[r, b - DEPTH : b, :] = jnp.where(at_right == 1, jnp.zeros_like(edge), edge)
                v, b = v[: b - DEPTH - a], b - DEPTH
            dst[r, a:b, :] = v
            return ctr, down

        def rows(i, pair):
            for j in range(unroll):
                pair = row(first + unroll * i + j, *pair)
            return pair

        pair = (src[first - 1, c0:c1, :], src[first, c0:c1, :])
        whole = count // unroll
        if whole > 1:
            pair = lax.fori_loop(0, whole, rows, pair)
        elif whole:
            pair = rows(0, pair)
        for r in range(first + whole * unroll, last):
            pair = row(r, *pair)


def halves(v):
    high = v.astype(jnp.bfloat16)
    low = (v - high.astype(jnp.float32)).astype(jnp.bfloat16)
    return jnp.concatenate([high, low], axis=1)


def fold(p):
    n, m = p.shape[0] // 2, p.shape[1] // 2
    return (p[:n, :m] + p[n:, m:]) + (p[:n, m:] + p[n:, :m])


def block_rows(buf, at, step, lanes_at, core):
    nm = buf.shape[2]

    def take(first, last):
        rows = buf[at + first * step : at + last * step, lanes_at : lanes_at + core, :]
        return halves(rows.reshape((last - first) * step * core, nm))

    return take


def add_gram(left, *pairs):
    right = jnp.concatenate([r for _, r in pairs], axis=1)
    p = lax.dot_general(
        left, right, (((0,), (0,)), ((), ())), preferred_element_type=jnp.float32
    )
    width = left.shape[1]
    for i, (dst, _) in enumerate(pairs):
        dst[...] += fold(p[:, i * width : (i + 1) * width])


def half_operator(x, weight, tmp, first, last, core):
    nm = x.shape[2]
    c0, c1 = 2 * DEPTH, 2 * DEPTH + core
    spot = lax.broadcasted_iota(jnp.int32, (DEPTH, nm), 0)
    for i in range(first, last):
        r = DEPTH + i
        for a, b in ((c0, c1 - DEPTH), (c1 - DEPTH, c1)):
            side = x[r, a + 1 : b + 1, :]
            if b == c1:
                side = jnp.where(spot == DEPTH - 1, 0.0, side)
            if i:
                side = side + x[r - 1, a:b, :]
            tmp[i - first, a - c0 : b - c0, :] = (
                0.25 * weight[r, a:b, :] * x[r, a:b, :] + 0.2 * side
            )


def finish_sums(x, weight, tmp, start, sums, first, last, core, opens):
    gram, ray, coup = sums
    field = block_rows(x, DEPTH, 1, 2 * DEPTH, core)(first, last)
    half_operator(x, weight, tmp, first, last, core)
    half = block_rows(tmp, 0, 1, 0, core)(0, last - first)
    opening = block_rows(start, 0, 1, 0, core)(first, last)
    add_gram(field, (gram, field), (ray, half), (coup, jnp.where(opens, opening, jnp.zeros_like(opening))))


def near_kernel(dims, pos, *refs):
    rows_here, group, wide, core = dims
    tall = rows_here * group
    known = tall + DEPTH
    n_near = group + group // 2
    at = 2 * group
    messages, refs = refs[:n_near], refs[n_near:]
    x, y, weight, start, gram1, gram2, ray, coup, cs, tmp = refs
    nm = x.shape[2]
    span = wide + 2 * DEPTH
    sign, col = pos[at], pl.multiple_of(pos[at + 1], 8)
    low, sides = pos[at + 2], (pos[at + 4], pos[at + 5])
    zero = jnp.zeros((2 * DEPTH, nm), jnp.float32)

    def clear(r, _):
        for buf in (x, y, weight):
            buf[r, 0 : 2 * DEPTH, :] = zero
            buf[r, span - 2 * DEPTH : span, :] = zero
        return 0

    lax.fori_loop(0, tall + 2 * DEPTH, clear, 0)
    blank = jnp.zeros((span, nm), jnp.float32)
    y[DEPTH - 1] = blank
    y[known] = blank
    spread(messages, (rows_here, wide), pos, col, 0, sign, x, weight, cs)
    for i in range(tall):
        start[i] = x[DEPTH + i, 2 * DEPTH : 2 * DEPTH + core, :]
    for total in (gram1, gram2, ray, coup):
        total[...] = jnp.zeros_like(total)
    take = block_rows(x, DEPTH, rows_here, 2 * DEPTH, core)
    for k in range(1, DEPTH + 1):
        dst, src = (y, x) if k % 2 else (x, y)
        opening = k % DEGREE == 1
        if k < DEPTH:

            @pl.when(low < DEPTH)
            def _(dst=dst, src=src, k=k, opening=opening):
                apply_rows(dst, src, weight, wide, sides, k, DEPTH, opening)

        apply_rows(dst, src, weight, wide, sides, DEPTH, known - k, opening)
        if k == DEGREE:
            f = take(0, group - DEGREE // rows_here)
            add_gram(f, (gram1, f))
    finish_sums(x, weight, tmp, start, (gram2, ray, coup), 0, tall // 2, core, pos[at + 6] == 1)


def far_kernel(dims, pos, *refs):
    rows_here, group, wide, core = dims
    tall = rows_here * group
    known = tall + DEPTH
    n_far = group // 2
    at = 2 * group
    messages, refs = refs[:n_far], refs[n_far:]
    start, gram1_in, gram2_in, ray_in, coup_in, refs = *refs[3:8], refs[8:]
    x, y, weight, packed, ray, coup, out, row0 = refs[:8]
    backs, (cs, tmp, gram1, gram2) = refs[8 : 7 + group], refs[7 + group :]
    sign, col = pos[at], pl.multiple_of(pos[at + 1], 8)
    high, sides = pos[at + 3], (pos[at + 4], pos[at + 5])
    spread(messages, (rows_here, wide), pos, col, group + group // 2, sign, x, weight, cs)
    for total, before in ((gram1, gram1_in), (gram2, gram2_in), (ray, ray_in), (coup, coup_in)):
        total[...] = before[...]
    take = block_rows(x, DEPTH, rows_here, 2 * DEPTH, core)
    for k in range(1, DEPTH + 1):
        dst, src = (y, x) if k % 2 else (x, y)
        opening = k % DEGREE == 1
        apply_rows(dst, src, weight, wide, sides, known - k, known, opening)
        if k < DEPTH:

            @pl.when(high > known)
            def _(dst=dst, src=src, k=k, opening=opening):
                apply_rows(dst, src, weight, wide, sides, known, known + DEPTH - k, opening)

        if k == DEGREE:
            f = take(group - DEGREE // rows_here, group)
            add_gram(f, (gram1, f))
    for i in range(tall):
        out[i] = x[DEPTH + i, 2 * DEPTH : 2 * DEPTH + core, :]
        for back in backs:
            at_end = rows_here * core + i
            back[at_end : at_end + 1, :] = x[DEPTH + i, 2 * DEPTH : 2 * DEPTH + 1, :]
    row0[...] = x[DEPTH + tall - 1, 2 * DEPTH : 2 * DEPTH + core, :]
    for k, back in enumerate(backs):
        for r in range(rows_here):
            back[r * core : (r + 1) * core, :] = x[
                DEPTH + pos[at + 7 + k] + r, 2 * DEPTH : 2 * DEPTH + core, :
            ]
    finish_sums(x, weight, tmp, start, (gram2, ray, coup), tall // 2, tall, core, pos[at + 6] == 1)
    half = gram1.shape[0] // 2
    lane = lax.broadcasted_iota(jnp.int32, (half, 2 * half), 1)
    packed[:half] = gram1[:half]
    packed[half : 2 * half] = gram2[:half]
    packed[2 * half :] = jnp.where(lane < half, pltpu.roll(gram2[half:], half, 1), gram1[half:])


def late_kernel(dims, turn, out, recv, down, ray0, coup0, *refs):
    rows_here, tall, core = dims
    columns, (ray, coup, side) = refs[:-3], refs[-3:]
    coup[...] = coup0[...]
    add_gram(
        block_rows(out, 0, 1, 0, core)(0, tall), (coup, block_rows(recv, 0, 1, 0, core)(0, tall))
    )
    for i in range(tall):
        total = jnp.zeros((1, side.shape[1]), jnp.float32)
        for k, column in enumerate(columns):
            there = column[pl.ds(rows_here * core + turn[0] + turn[1] * i, 1), :]
            total = jnp.where(turn[2 + k] == 1, there, total)
        side[i : i + 1, :] = total
    ray[...] = ray0[...] + 0.2 * (
        mm_t(out[0], down[...]) + mm_t(out[:, core - 1, :], side[...])
    )


def modes_kernel(dims, pos, *refs):
    rows_here, group, core = dims
    blocks, (mix, modes, rows, sem) = refs[:group], refs[group:]
    nm = mix.shape[0]
    m = halves(mix[...])
    m = jnp.concatenate([m, m], axis=0)
    copies = []
    for r in range(rows_here):
        for k in range(group):
            at = pl.multiple_of(pos[3 * k] * core, core)
            row = pos[3 * k + 1] + pos[3 * k + 2] * r
            if k:
                v = blocks[k][pl.ds(pl.multiple_of(row * core, core), core), :]
            else:
                v = blocks[k][row]
            p = jnp.dot(halves(v), m, preferred_element_type=jnp.float32)
            rows[r, pl.ds(at, core), :] = p[:, :nm] + p[:, nm:]
        copies.append(pltpu.make_async_copy(rows.at[r], modes.at[r], sem.at[r]))
        copies[-1].start()
    for c in copies:
        c.wait()


SUB = 8


def inverse_factor(a, work, panel):
    n, big = a.shape[0], panel.shape[0]
    work[...] = a
    full = (SUB, n)
    lane = lax.broadcasted_iota(jnp.int32, full, 1)
    sub = lax.broadcasted_iota(jnp.int32, full, 0)
    for top in range(0, n, big):
        blocks = [work[at : at + SUB, :] for at in range(top, top + big, SUB)]
        for j in range(big // SUB):
            at = top + j * SUB
            diag = blocks[j]
            e = {
                (i, k): jnp.broadcast_to(diag[i : i + 1, at + k : at + k + 1], full)
                for i in range(SUB)
                for k in range(i + 1)
            }
            low, inv = {}, []
            for k in range(SUB):
                inv.append(lax.rsqrt(e[k, k]))
                for i in range(k + 1, SUB):
                    low[i, k] = e[i, k] * inv[k]
                for m in range(k + 1, SUB):
                    for i in range(m, SUB):
                        e[i, m] = e[i, m] - low[i, k] * low[m, k]
            here = (lane >= at) & (lane < at + SUB)
            unit = jnp.where(lane == at + sub, 1.0, 0.0)
            diag = jnp.where(here, unit, diag)
            ups = []
            for k in range(SUB):
                row = jnp.broadcast_to(diag[k : k + 1, :], full)
                for m in range(k):
                    row = row - low[k, m] * ups[m]
                ups.append(row * inv[k])
            done = ups[0]
            for k in range(1, SUB):
                done = jnp.where(sub == k, ups[k], done)
            blocks[j] = done
            for i in range(j + 1, big // SUB):
                cols = []
                for k in range(SUB):
                    c = jnp.broadcast_to(blocks[i][:, at + k : at + k + 1], full)
                    for m in range(k):
                        c = c - low[k, m] * cols[m]
                    cols.append(c * inv[k])
                rest = jnp.where(here, 0.0, blocks[i])
                for k in range(SUB):
                    rest = rest - cols[k] * ups[k]
                blocks[i] = rest
        for j in range(big // SUB):
            at = top + j * SUB
            work[at : at + SUB, :] = blocks[j]
            panel[j * SUB : (j + 1) * SUB, :] = blocks[j]
        if top + big < n:
            done = panel[...]
            r = lax.broadcasted_iota(jnp.int32, done.shape, 0) + top
            c = lax.broadcasted_iota(jnp.int32, done.shape, 1)
            fix = mm_t(done, jnp.where((c > r) & (c < top + big), 0.0, done))
            old = work[top + big :, :]
            spot = lax.broadcasted_iota(jnp.int32, old.shape, 1)
            old = jnp.where((spot >= top) & (spot < top + big), 0.0, old)
            work[top + big :, :] = old - fix[top + big :, :]
    row = lax.broadcasted_iota(jnp.int32, (n, n), 0)
    column = lax.broadcasted_iota(jnp.int32, (n, n), 1)
    work[...] = jnp.where(column <= row, work[...], 0.0)


def turn_kernel(rot, order, turned):
    nm = rot.shape[1]
    ids = lax.broadcasted_iota(jnp.int32, (nm, nm), 0)
    for t in range(rot.shape[0]):
        turned[t] = mm(rot[t], (order[t : t + 1, :] == ids).astype(jnp.float32))


def mixing_kernel(scale, packed, there, turned, mix, work, panel, gram):
    n = mix.shape[0]
    half = n // 2

    def unpack(t):
        at = t * half
        upper = (packed[at : at + half, :] + there[at : at + half, :]) * scale
        rest = (packed[2 * half :, :] + there[2 * half :, :]) * scale
        if t:
            rest = pltpu.roll(rest, half, 1)
        gram[:half, :] = upper
        gram[half:, :] = rest
        gram[half:, :half] = upper.T[half:, :]
        return gram[...]

    inverse_factor(unpack(0), work, panel)
    m1 = mm_t(work[...], turned[0])
    inverse_factor(mm_t(m1, mm(unpack(1), m1)), work, panel)
    m2 = mm_t(work[...], turned[1])
    mix[...] = mm(m1, m2)


def reversed_bits(value, count):
    out = 0
    while count > 1:
        out, value, count = 2 * out + value % 2, value // 2, count // 2
    return out


def project_kernel(peers, scale, first, ray, coup, before, mix, shares):
    nm = mix.shape[0]
    share = nm // peers
    m = mix[...] * scale

    def place(value, at):
        for r in range(peers):
            to = (2 * reversed_bits(r, peers) + at) * share
            shares[to : to + share, :] = value[r * share : (r + 1) * share, :]

    place(mm_t(mix[...], mm(ray[...] + ray[...].T, m)), 1)
    half = mm_t(coup[...], m)

    @pl.when(first[0] == 1)
    def _():
        place(half, 0)

    @pl.when(first[0] != 1)
    def _():
        place(mm_t(before[...], half), 0)


def scatter_sum(value, axis):
    peers = lax.axis_size(axis)
    me = lax.axis_index(axis)
    bit = 1
    while bit < peers:
        half = value.shape[0] // 2
        odd = (me & bit) != 0
        low, high = value[:half], value[half:]
        other = xor_swap(jnp.where(odd, low, high), axis, bit)
        value = jnp.where(odd, high, low) + other
        bit *= 2
    return value


def xor_swap(value, axis, bit):
    peers = lax.axis_size(axis)
    return lax.ppermute(value, axis, [(i, i ^ bit) for i in range(peers)])


def sum_over(value, axis):
    peers = lax.axis_size(axis)
    bit = 1
    while bit < peers:
        there = xor_swap(value, axis, bit)
        bit *= 2
        if bit < peers:
            value = value + there
    return value, there


def body(start_modes, contrast, rotations, ordering):
    v0, section = start_modes[0], contrast[0]
    rows_here, columns, nm = v0.shape
    peers = lax.axis_size("rows")
    cuts = lax.axis_size("cuts")
    near = DEPTH // rows_here
    group = 2 * near
    core = columns // group
    wide = core + 2 * DEPTH
    tall = group * rows_here
    pixels = rows_here * peers * columns
    me = lax.axis_index("rows")
    cut = lax.axis_index("cuts")
    q = me % group
    block = me // group
    blocks = peers // group

    def hop(j, relayed=False):
        pairs = []
        for i in range(peers):
            z, s = i // group, i % group
            to = z + 1 if (s >= near) != relayed else z - 1
            if 0 <= to < blocks:
                pairs.append((i, to * group + (s ^ j)))
        return pairs

    def window(k):
        at = jnp.clip((q ^ k) * core - DEPTH, 0, columns - wide)
        part = lax.dynamic_slice(v0, (0, at, 0), (rows_here, wide, nm)).reshape(-1, nm)
        tail = lax.dynamic_slice(section, (0, at), (rows_here, wide))
        tail = jnp.pad(tail, ((0, 0), (0, 2 * LANES - wide))).reshape(2 * rows_here, LANES)
        return jnp.concatenate([part, tail], axis=0)

    vmem = pl.BlockSpec(memory_space=pltpu.VMEM)
    smem = pl.BlockSpec(memory_space=pltpu.SMEM)
    hbm = pl.BlockSpec(memory_space=pltpu.HBM)
    windows = [window(k) for k in range(group)]
    arrived = [None] * group
    for k in reversed(range(1, group)):
        arrived[k] = xor_swap(windows[k], "rows", k)
    direct = []
    for j in range(near):
        direct.append(lax.ppermute(windows[j], "rows", hop(j)))
    relay = [lax.ppermute(arrived[k], "rows", hop(0, True)) for k in range(near, group)]
    messages = [windows[0]] + arrived[1:] + direct + relay

    lower = q >= near
    total = tall + 2 * DEPTH
    sign = jnp.where(lower, 1, -1)
    image = [DEPTH + (q ^ k) * rows_here for k in range(group)]
    for j in range(near):
        s = q ^ j
        image.append(jnp.where(lower, (s - near) * rows_here, DEPTH + tall + s * rows_here))
    for k in range(near, group):
        s = q ^ k
        image.append(jnp.where(lower, DEPTH + tall + s * rows_here, (s - near) * rows_here))
    at = jnp.clip(q * core - DEPTH, 0, columns - wide)
    top, bottom = block == 0, block == blocks - 1
    no_near = jnp.where(lower, top, bottom)
    no_far = jnp.where(lower, bottom, top)
    place = [jnp.where(lower, i, total - 1 - i) for i in image] + [
        sign,
        DEPTH + at - (q * core - DEPTH),
        jnp.where(no_near, DEPTH, 0),
        jnp.where(no_far, DEPTH + tall, total),
        q == 0,
        q == group - 1,
        cut == 0,
    ]
    for k in range(1, group):
        s = (q ^ k) * rows_here
        place.append(jnp.where(lower, s, tall - rows_here - s))
    place = jnp.stack([jnp.asarray(p, jnp.int32) for p in place])

    square = jax.ShapeDtypeStruct((nm, nm), jnp.float32)
    tile = jax.ShapeDtypeStruct((tall, core, nm), jnp.float32)
    span = wide + 2 * DEPTH
    field_buffer = jax.ShapeDtypeStruct((total, span, nm), jnp.float32)

    def grant(mib):
        return pltpu.CompilerParams(vmem_limit_bytes=mib * 1024 * 1024)

    params = grant(10)
    dims = (rows_here, group, wide, core)
    early, far = messages[: group + near], messages[group + near :]
    x, y, weight, start, *sums = pl.pallas_call(
        functools.partial(near_kernel, dims),
        out_shape=(field_buffer,) * 3
        + (tile,)
        + (square,) * 4,
        in_specs=[smem] + [vmem] * len(early),
        out_specs=[vmem] * 8,
        scratch_shapes=[
            pltpu.VMEM((2 * rows_here * len(early), LANES), jnp.float32),
            pltpu.VMEM((tall // 2, core, nm), jnp.float32),
        ],
        compiler_params=params,
        cost_estimate=pl.CostEstimate(flops=10**9, bytes_accessed=4 * 10**7, transcendentals=0),
        name="near",
    )(place, *early)
    n_far = len(far)
    back_block = jax.ShapeDtypeStruct((rows_here * core + tall, nm), jnp.float32)
    packed = jax.ShapeDtypeStruct((3 * nm // 2, nm), jnp.float32)
    _, _, _, packed, ray, coup, field, row0, *back = pl.pallas_call(
        functools.partial(far_kernel, dims),
        out_shape=(field_buffer,) * 3
        + (packed,)
        + (square,) * 2
        + (tile, jax.ShapeDtypeStruct((core, nm), jnp.float32))
        + (back_block,) * (group - 1),
        in_specs=[smem] + [vmem] * (n_far + 8),
        out_specs=[vmem] * (7 + group),
        input_output_aliases={1 + n_far + i: i for i in range(3)},
        scratch_shapes=[
            pltpu.VMEM((2 * rows_here * n_far, LANES), jnp.float32),
            pltpu.VMEM((tall // 2, core, nm), jnp.float32),
            pltpu.VMEM((nm, nm), jnp.float32),
            pltpu.VMEM((nm, nm), jnp.float32),
        ],
        compiler_params=params,
        cost_estimate=pl.CostEstimate(flops=10**9, bytes_accessed=2 * 10**7, transcendentals=0),
        name="far",
    )(place, *far, x, y, weight, start, *sums)

    recv = lax.ppermute(field, "cuts", [(i, i + 1) for i in range(cuts - 1)])
    packed, packed_there = sum_over(packed, "rows")
    down = lax.ppermute(row0, "rows", hop(0))
    sent = back
    back = []
    for k in range(1, group):
        back.append(xor_swap(sent[k - 1], "rows", k))

    turned = pl.pallas_call(
        turn_kernel,
        out_shape=jax.ShapeDtypeStruct(rotations.shape[1:], jnp.float32),
        in_specs=[vmem] * 2,
        out_specs=vmem,
        compiler_params=grant(2),
        cost_estimate=pl.CostEstimate(flops=10**8, bytes_accessed=10**6, transcendentals=0),
        name="turn",
    )(rotations[0], ordering[0])
    big = min(nm, 64)
    mix = pl.pallas_call(
        functools.partial(mixing_kernel, 1.0 / pixels),
        out_shape=square,
        in_specs=[vmem] * 3,
        out_specs=vmem,
        compiler_params=grant(4),
        cost_estimate=pl.CostEstimate(flops=10**9, bytes_accessed=4 * 10**7, transcendentals=0),
        scratch_shapes=[
            pltpu.VMEM((nm, nm), jnp.float32),
            pltpu.VMEM((big, nm), jnp.float32),
            pltpu.VMEM((nm, nm), jnp.float32),
        ],
        name="mixing",
    )(packed, packed_there, turned)

    before = lax.ppermute(mix, "cuts", [(i, i + 1) for i in range(cuts - 1)])
    edges = [k for k in range(1, group) if k & (k + 1) == 0]
    beside = [back[k - 1] for k in edges]
    recv, down, beside, mix_now = lax.optimization_barrier((recv, down, beside, mix))
    flip = q == near - 1
    turn = [jnp.where(flip, tall - 1, 0), jnp.where(flip, -1, 1)]
    turn += [(((q ^ (q + 1)) == k) & (q != group - 1)).astype(jnp.int32) for k in edges]
    turn = jnp.stack(turn)
    ray, coup = pl.pallas_call(
        functools.partial(late_kernel, (rows_here, tall, core)),
        out_shape=(square, square),
        in_specs=[smem] + [vmem] * (5 + len(edges)),
        out_specs=[vmem] * 2,
        scratch_shapes=[pltpu.VMEM((tall, nm), jnp.float32)],
        compiler_params=grant(6),
        cost_estimate=pl.CostEstimate(flops=10**9, bytes_accessed=10**7, transcendentals=0),
        name="late",
    )(turn.astype(jnp.int32), field, recv, down, ray, coup, *beside)
    share = nm // peers
    first = (cut == 0).astype(jnp.int32).reshape(1)
    shares = pl.pallas_call(
        functools.partial(project_kernel, peers, 1.0 / pixels),
        out_shape=jax.ShapeDtypeStruct((2 * nm, nm), jnp.float32),
        in_specs=[smem] + [vmem] * 4,
        out_specs=vmem,
        compiler_params=grant(4),
        cost_estimate=pl.CostEstimate(flops=10**8, bytes_accessed=10**6, transcendentals=0),
        name="project",
    )(first, ray, coup, before, mix_now)
    shares = scatter_sum(shares, "rows")
    coupling, rayleigh = shares[:share], shares[share:]

    where = []
    for k in range(group):
        source = q ^ k
        base = 0
        if k == 0:
            base = jnp.where(lower, q * rows_here, tall - rows_here - q * rows_here)
        down_there = source >= near
        where += [
            source,
            jnp.where(down_there, base, base + rows_here - 1),
            jnp.where(down_there, 1, -1),
        ]
    where = jnp.stack([jnp.asarray(p, jnp.int32) for p in where])
    modes = pl.pallas_call(
        functools.partial(modes_kernel, (rows_here, group, core)),
        out_shape=jax.ShapeDtypeStruct((rows_here, columns, nm), jnp.float32),
        in_specs=[smem] + [vmem] * (group + 1),
        out_specs=hbm,
        scratch_shapes=[
            pltpu.VMEM((rows_here, columns, nm), jnp.float32),
            pltpu.SemaphoreType.DMA((rows_here,)),
        ],
        compiler_params=grant(6),
        cost_estimate=pl.CostEstimate(flops=10**9, bytes_accessed=10**7, transcendentals=0),
        name="modes",
    )(where, field, *back, mix)
    return modes[None], coupling[None], rayleigh[None]


def solution(mesh):
    placed = (
        P("cuts", "rows", None, None),
        P("cuts", "rows", None),
        P("cuts", None, None, None),
        P("cuts", None, None),
    )

    return jax.shard_map(
        body,
        mesh=mesh,
        in_specs=placed,
        out_specs=(P("cuts", "rows", None, None), P("cuts", "rows", None), P("cuts", "rows", None)),
        check_vma=False,
    )
```

```python
import functools

import jax
import jax.numpy as jnp
from jax import lax
from jax.experimental import pallas as pl
from jax.experimental.pallas import tpu as pltpu
from jax.sharding import PartitionSpec as P


DEGREE = 4
ITERS = 2
DEPTH = DEGREE * ITERS
LANES = 128
HIGHEST = lax.Precision.HIGHEST


def mm(a, b):
    return jnp.dot(a, b, precision=HIGHEST, preferred_element_type=jnp.float32)


def mm_t(a, b):
    return lax.dot_general(
        a, b, (((0,), (0,)), ((), ())), precision=HIGHEST, preferred_element_type=jnp.float32
    )


def spread(messages, dims, pos, col, at, sign, x, weight, cs):
    rows_here, wide = dims
    nm = x.shape[2]
    for i, message in enumerate(messages):
        for r in range(rows_here):
            x[pos[at + i] + sign * r, pl.ds(col, wide), :] = message[r * wide : (r + 1) * wide, :]
        cs[2 * rows_here * i : 2 * rows_here * (i + 1), :] = message[rows_here * wide :, :]
    turned = (1.6 * cs[...] - 0.4).T
    for i in range(len(messages)):
        for r in range(rows_here):
            row = pos[at + i] + sign * r
            c = 2 * (rows_here * i + r)
            weight[row, pl.ds(col, LANES), :] = jnp.broadcast_to(
                turned[:, c : c + 1], (LANES, nm)
            )
            weight[row, pl.ds(pl.multiple_of(col + LANES, 8), wide - LANES), :] = (
                jnp.broadcast_to(turned[: wide - LANES, c + 1 : c + 2], (wide - LANES, nm))
            )


def apply_rows(dst, src, weight, wide, sides, first, last, opening):
    left = DEPTH
    at_left, at_right = sides
    count = last - first
    strip = wide // 3 if wide % 24 == 0 else wide
    unroll = 4

    for c0 in range(left, left + wide, strip):
        c1 = c0 + strip

        def row(r, up, ctr, c0=c0, c1=c1):
            down = src[r + 1, c0:c1, :]
            s = (up + down) + (src[r, c0 - 1 : c1 - 1, :] + src[r, c0 + 1 : c1 + 1, :])
            v = weight[r, c0:c1, :] * ctr + 0.4 * s
            if opening:
                v = 0.5 * v
            else:
                v = v - dst[r, c0:c1, :]
            a, b = c0, c1
            if c0 == left:
                edge = v[:DEPTH]
                dst[r, a : a + DEPTH, :] = jnp.where(at_left == 1, jnp.zeros_like(edge), edge)
                v, a = v[DEPTH:], a + DEPTH
            if c1 == left + wide:
                edge = v[b - DEPTH - a :]
                dst[r, b - DEPTH : b, :] = jnp.where(at_right == 1, jnp.zeros_like(edge), edge)
                v, b = v[: b - DEPTH - a], b - DEPTH
            dst[r, a:b, :] = v
            return ctr, down

        def rows(i, pair):
            for j in range(unroll):
                pair = row(first + unroll * i + j, *pair)
            return pair

        pair = (src[first - 1, c0:c1, :], src[first, c0:c1, :])
        whole = count // unroll
        if whole > 1:
            pair = lax.fori_loop(0, whole, rows, pair)
        elif whole:
            pair = rows(0, pair)
        for r in range(first + whole * unroll, last):
            pair = row(r, *pair)


def halves(v):
    high = v.astype(jnp.bfloat16)
    low = (v - high.astype(jnp.float32)).astype(jnp.bfloat16)
    return jnp.concatenate([high, low], axis=1)


def fold(p):
    n, m = p.shape[0] // 2, p.shape[1] // 2
    return (p[:n, :m] + p[n:, m:]) + (p[:n, m:] + p[n:, :m])


def block_rows(buf, at, step, lanes_at, core):
    nm = buf.shape[2]

    def take(first, last):
        rows = buf[at + first * step : at + last * step, lanes_at : lanes_at + core, :]
        return halves(rows.reshape((last - first) * step * core, nm))

    return take


def add_gram(left, *pairs):
    right = jnp.concatenate([r for _, r in pairs], axis=1)
    p = lax.dot_general(
        left, right, (((0,), (0,)), ((), ())), preferred_element_type=jnp.float32
    )
    width = left.shape[1]
    for i, (dst, _) in enumerate(pairs):
        dst[...] += fold(p[:, i * width : (i + 1) * width])


def half_operator(x, weight, tmp, first, last, core):
    nm = x.shape[2]
    c0, c1 = 2 * DEPTH, 2 * DEPTH + core
    spot = lax.broadcasted_iota(jnp.int32, (DEPTH, nm), 0)
    for i in range(first, last):
        r = DEPTH + i
        for a, b in ((c0, c1 - DEPTH), (c1 - DEPTH, c1)):
            side = x[r, a + 1 : b + 1, :]
            if b == c1:
                side = jnp.where(spot == DEPTH - 1, 0.0, side)
            if i:
                side = side + x[r - 1, a:b, :]
            tmp[i - first, a - c0 : b - c0, :] = (
                0.25 * weight[r, a:b, :] * x[r, a:b, :] + 0.2 * side
            )


def finish_sums(x, weight, tmp, start, sums, first, last, core, opens):
    gram, ray, coup = sums
    field = block_rows(x, DEPTH, 1, 2 * DEPTH, core)(first, last)
    half_operator(x, weight, tmp, first, last, core)
    half = block_rows(tmp, 0, 1, 0, core)(0, last - first)
    opening = block_rows(start, 0, 1, 0, core)(first, last)
    add_gram(field, (gram, field), (ray, half), (coup, jnp.where(opens, opening, jnp.zeros_like(opening))))


def near_kernel(dims, pos, *refs):
    rows_here, group, wide, core = dims
    tall = rows_here * group
    known = tall + DEPTH
    n_near = group + group // 2
    at = 2 * group
    messages, refs = refs[:n_near], refs[n_near:]
    x, y, weight, start, gram1, gram2, ray, coup, cs, tmp = refs
    nm = x.shape[2]
    span = wide + 2 * DEPTH
    sign, col = pos[at], pl.multiple_of(pos[at + 1], 8)
    low, sides = pos[at + 2], (pos[at + 4], pos[at + 5])
    zero = jnp.zeros((2 * DEPTH, nm), jnp.float32)

    def clear(r, _):
        for buf in (x, y, weight):
            buf[r, 0 : 2 * DEPTH, :] = zero
            buf[r, span - 2 * DEPTH : span, :] = zero
        return 0

    lax.fori_loop(0, tall + 2 * DEPTH, clear, 0)
    blank = jnp.zeros((span, nm), jnp.float32)
    y[DEPTH - 1] = blank
    y[known] = blank
    spread(messages, (rows_here, wide), pos, col, 0, sign, x, weight, cs)
    for i in range(tall):
        start[i] = x[DEPTH + i, 2 * DEPTH : 2 * DEPTH + core, :]
    for total in (gram1, gram2, ray, coup):
        total[...] = jnp.zeros_like(total)
    take = block_rows(x, DEPTH, rows_here, 2 * DEPTH, core)
    for k in range(1, DEPTH + 1):
        dst, src = (y, x) if k % 2 else (x, y)
        opening = k % DEGREE == 1
        if k < DEPTH:

            @pl.when(low < DEPTH)
            def _(dst=dst, src=src, k=k, opening=opening):
                apply_rows(dst, src, weight, wide, sides, k, DEPTH, opening)

        apply_rows(dst, src, weight, wide, sides, DEPTH, known - k, opening)
        if k == DEGREE:
            f = take(0, group - DEGREE // rows_here)
            add_gram(f, (gram1, f))
    finish_sums(x, weight, tmp, start, (gram2, ray, coup), 0, tall // 2, core, pos[at + 6] == 1)


def far_kernel(dims, pos, *refs):
    rows_here, group, wide, core = dims
    tall = rows_here * group
    known = tall + DEPTH
    n_far = group // 2
    at = 2 * group
    messages, refs = refs[:n_far], refs[n_far:]
    start, gram1_in, gram2_in, ray_in, coup_in, refs = *refs[3:8], refs[8:]
    x, y, weight, packed, ray, coup, out, row0 = refs[:8]
    backs, (cs, tmp, gram1, gram2) = refs[8 : 7 + group], refs[7 + group :]
    sign, col = pos[at], pl.multiple_of(pos[at + 1], 8)
    high, sides = pos[at + 3], (pos[at + 4], pos[at + 5])
    spread(messages, (rows_here, wide), pos, col, group + group // 2, sign, x, weight, cs)
    for total, before in ((gram1, gram1_in), (gram2, gram2_in), (ray, ray_in), (coup, coup_in)):
        total[...] = before[...]
    take = block_rows(x, DEPTH, rows_here, 2 * DEPTH, core)
    for k in range(1, DEPTH + 1):
        dst, src = (y, x) if k % 2 else (x, y)
        opening = k % DEGREE == 1
        apply_rows(dst, src, weight, wide, sides, known - k, known, opening)
        if k < DEPTH:

            @pl.when(high > known)
            def _(dst=dst, src=src, k=k, opening=opening):
                apply_rows(dst, src, weight, wide, sides, known, known + DEPTH - k, opening)

        if k == DEGREE:
            f = take(group - DEGREE // rows_here, group)
            add_gram(f, (gram1, f))
    for i in range(tall):
        out[i] = x[DEPTH + i, 2 * DEPTH : 2 * DEPTH + core, :]
        for back in backs:
            at_end = rows_here * core + i
            back[at_end : at_end + 1, :] = x[DEPTH + i, 2 * DEPTH : 2 * DEPTH + 1, :]
    row0[...] = x[DEPTH + tall - 1, 2 * DEPTH : 2 * DEPTH + core, :]
    for k, back in enumerate(backs):
        for r in range(rows_here):
            back[r * core : (r + 1) * core, :] = x[
                DEPTH + pos[at + 7 + k] + r, 2 * DEPTH : 2 * DEPTH + core, :
            ]
    finish_sums(x, weight, tmp, start, (gram2, ray, coup), tall // 2, tall, core, pos[at + 6] == 1)
    half = gram1.shape[0] // 2
    lane = lax.broadcasted_iota(jnp.int32, (half, 2 * half), 1)
    packed[:half] = gram1[:half]
    packed[half : 2 * half] = gram2[:half]
    packed[2 * half :] = jnp.where(lane < half, pltpu.roll(gram2[half:], half, 1), gram1[half:])


def late_kernel(dims, turn, out, recv, down, ray0, coup0, *refs):
    rows_here, tall, core = dims
    columns, (ray, coup, side) = refs[:-3], refs[-3:]
    coup[...] = coup0[...]
    add_gram(
        block_rows(out, 0, 1, 0, core)(0, tall), (coup, block_rows(recv, 0, 1, 0, core)(0, tall))
    )
    for i in range(tall):
        total = jnp.zeros((1, side.shape[1]), jnp.float32)
        for k, column in enumerate(columns):
            there = column[pl.ds(rows_here * core + turn[0] + turn[1] * i, 1), :]
            total = jnp.where(turn[2 + k] == 1, there, total)
        side[i : i + 1, :] = total
    ray[...] = ray0[...] + 0.2 * (
        mm_t(out[0], down[...]) + mm_t(out[:, core - 1, :], side[...])
    )


def modes_kernel(dims, pos, *refs):
    rows_here, group, core = dims
    blocks, (mix, modes, rows, sem) = refs[:group], refs[group:]
    nm = mix.shape[0]
    m = halves(mix[...])
    m = jnp.concatenate([m, m], axis=0)
    copies = []
    for r in range(rows_here):
        for k in range(group):
            at = pl.multiple_of(pos[3 * k] * core, core)
            row = pos[3 * k + 1] + pos[3 * k + 2] * r
            if k:
                v = blocks[k][pl.ds(pl.multiple_of(row * core, core), core), :]
            else:
                v = blocks[k][row]
            p = jnp.dot(halves(v), m, preferred_element_type=jnp.float32)
            rows[r, pl.ds(at, core), :] = p[:, :nm] + p[:, nm:]
        copies.append(pltpu.make_async_copy(rows.at[r], modes.at[r], sem.at[r]))
        copies[-1].start()
    for c in copies:
        c.wait()


SUB = 8


def inverse_factor(a, work, panel):
    n, big = a.shape[0], panel.shape[0]
    work[...] = a
    full = (SUB, n)
    lane = lax.broadcasted_iota(jnp.int32, full, 1)
    sub = lax.broadcasted_iota(jnp.int32, full, 0)
    for top in range(0, n, big):
        blocks = [work[at : at + SUB, :] for at in range(top, top + big, SUB)]
        for j in range(big // SUB):
            at = top + j * SUB
            diag = blocks[j]
            e = {
                (i, k): jnp.broadcast_to(diag[i : i + 1, at + k : at + k + 1], full)
                for i in range(SUB)
                for k in range(i + 1)
            }
            low, inv = {}, []
            for k in range(SUB):
                inv.append(lax.rsqrt(e[k, k]))
                for i in range(k + 1, SUB):
                    low[i, k] = e[i, k] * inv[k]
                for m in range(k + 1, SUB):
                    for i in range(m, SUB):
                        e[i, m] = e[i, m] - low[i, k] * low[m, k]
            here = (lane >= at) & (lane < at + SUB)
            unit = jnp.where(lane == at + sub, 1.0, 0.0)
            diag = jnp.where(here, unit, diag)
            ups = []
            for k in range(SUB):
                row = jnp.broadcast_to(diag[k : k + 1, :], full)
                for m in range(k):
                    row = row - low[k, m] * ups[m]
                ups.append(row * inv[k])
            done = ups[0]
            for k in range(1, SUB):
                done = jnp.where(sub == k, ups[k], done)
            blocks[j] = done
            for i in range(j + 1, big // SUB):
                cols = []
                for k in range(SUB):
                    c = jnp.broadcast_to(blocks[i][:, at + k : at + k + 1], full)
                    for m in range(k):
                        c = c - low[k, m] * cols[m]
                    cols.append(c * inv[k])
                rest = jnp.where(here, 0.0, blocks[i])
                for k in range(SUB):
                    rest = rest - cols[k] * ups[k]
                blocks[i] = rest
        for j in range(big // SUB):
            at = top + j * SUB
            work[at : at + SUB, :] = blocks[j]
            panel[j * SUB : (j + 1) * SUB, :] = blocks[j]
        if top + big < n:
            done = panel[...]
            r = lax.broadcasted_iota(jnp.int32, done.shape, 0) + top
            c = lax.broadcasted_iota(jnp.int32, done.shape, 1)
            fix = mm_t(done, jnp.where((c > r) & (c < top + big), 0.0, done))
            old = work[top + big :, :]
            spot = lax.broadcasted_iota(jnp.int32, old.shape, 1)
            old = jnp.where((spot >= top) & (spot < top + big), 0.0, old)
            work[top + big :, :] = old - fix[top + big :, :]
    row = lax.broadcasted_iota(jnp.int32, (n, n), 0)
    column = lax.broadcasted_iota(jnp.int32, (n, n), 1)
    work[...] = jnp.where(column <= row, work[...], 0.0)


def turn_kernel(rot, order, turned):
    nm = rot.shape[1]
    ids = lax.broadcasted_iota(jnp.int32, (nm, nm), 0)
    for t in range(rot.shape[0]):
        turned[t] = mm(rot[t], (order[t : t + 1, :] == ids).astype(jnp.float32))


def mixing_kernel(scale, packed, there, turned, mix, work, panel, gram):
    n = mix.shape[0]
    half = n // 2

    def unpack(t):
        at = t * half
        upper = (packed[at : at + half, :] + there[at : at + half, :]) * scale
        rest = (packed[2 * half :, :] + there[2 * half :, :]) * scale
        if t:
            rest = pltpu.roll(rest, half, 1)
        gram[:half, :] = upper
        gram[half:, :] = rest
        gram[half:, :half] = upper.T[half:, :]
        return gram[...]

    inverse_factor(unpack(0), work, panel)
    m1 = mm_t(work[...], turned[0])
    inverse_factor(mm_t(m1, mm(unpack(1), m1)), work, panel)
    m2 = mm_t(work[...], turned[1])
    mix[...] = mm(m1, m2)


def project_kernel(peers, scale, first, ray, coup, before, mix, shares):
    nm = mix.shape[0]
    share = nm // peers
    m = mix[...] * scale

    def place(value, at):
        for r in range(peers):
            to = (2 * r + at) * share
            shares[to : to + share, :] = value[r * share : (r + 1) * share, :]

    place(mm_t(mix[...], mm(ray[...] + ray[...].T, m)), 1)
    half = mm_t(coup[...], m)

    @pl.when(first[0] == 1)
    def _():
        place(half, 0)

    @pl.when(first[0] != 1)
    def _():
        place(mm_t(before[...], half), 0)


def xor_swap(value, axis, bit):
    peers = lax.axis_size(axis)
    return lax.ppermute(value, axis, [(i, i ^ bit) for i in range(peers)])


def sum_over(value, axis):
    peers = lax.axis_size(axis)
    bit = 1
    while bit < peers:
        there = xor_swap(value, axis, bit)
        bit *= 2
        if bit < peers:
            value = value + there
    return value, there


def body(start_modes, contrast, rotations, ordering):
    v0, section = start_modes[0], contrast[0]
    rows_here, columns, nm = v0.shape
    peers = lax.axis_size("rows")
    cuts = lax.axis_size("cuts")
    near = DEPTH // rows_here
    group = 2 * near
    core = columns // group
    wide = core + 2 * DEPTH
    tall = group * rows_here
    pixels = rows_here * peers * columns
    me = lax.axis_index("rows")
    cut = lax.axis_index("cuts")
    q = me % group
    block = me // group
    blocks = peers // group

    def hop(j, relayed=False):
        pairs = []
        for i in range(peers):
            z, s = i // group, i % group
            to = z + 1 if (s >= near) != relayed else z - 1
            if 0 <= to < blocks:
                pairs.append((i, to * group + (s ^ j)))
        return pairs

    def window(k):
        at = jnp.clip((q ^ k) * core - DEPTH, 0, columns - wide)
        part = lax.dynamic_slice(v0, (0, at, 0), (rows_here, wide, nm)).reshape(-1, nm)
        tail = lax.dynamic_slice(section, (0, at), (rows_here, wide))
        tail = jnp.pad(tail, ((0, 0), (0, 2 * LANES - wide))).reshape(2 * rows_here, LANES)
        return jnp.concatenate([part, tail], axis=0)

    vmem = pl.BlockSpec(memory_space=pltpu.VMEM)
    smem = pl.BlockSpec(memory_space=pltpu.SMEM)
    hbm = pl.BlockSpec(memory_space=pltpu.HBM)
    windows = [window(k) for k in range(group)]
    arrived = [None] * group
    for k in reversed(range(1, group)):
        arrived[k] = xor_swap(windows[k], "rows", k)
    direct = []
    for j in range(near):
        direct.append(lax.ppermute(windows[j], "rows", hop(j)))
    relay = [lax.ppermute(arrived[k], "rows", hop(0, True)) for k in range(near, group)]
    messages = [windows[0]] + arrived[1:] + direct + relay

    lower = q >= near
    total = tall + 2 * DEPTH
    sign = jnp.where(lower, 1, -1)
    image = [DEPTH + (q ^ k) * rows_here for k in range(group)]
    for j in range(near):
        s = q ^ j
        image.append(jnp.where(lower, (s - near) * rows_here, DEPTH + tall + s * rows_here))
    for k in range(near, group):
        s = q ^ k
        image.append(jnp.where(lower, DEPTH + tall + s * rows_here, (s - near) * rows_here))
    at = jnp.clip(q * core - DEPTH, 0, columns - wide)
    top, bottom = block == 0, block == blocks - 1
    no_near = jnp.where(lower, top, bottom)
    no_far = jnp.where(lower, bottom, top)
    place = [jnp.where(lower, i, total - 1 - i) for i in image] + [
        sign,
        DEPTH + at - (q * core - DEPTH),
        jnp.where(no_near, DEPTH, 0),
        jnp.where(no_far, DEPTH + tall, total),
        q == 0,
        q == group - 1,
        cut == 0,
    ]
    for k in range(1, group):
        s = (q ^ k) * rows_here
        place.append(jnp.where(lower, s, tall - rows_here - s))
    place = jnp.stack([jnp.asarray(p, jnp.int32) for p in place])

    square = jax.ShapeDtypeStruct((nm, nm), jnp.float32)
    tile = jax.ShapeDtypeStruct((tall, core, nm), jnp.float32)
    span = wide + 2 * DEPTH
    field_buffer = jax.ShapeDtypeStruct((total, span, nm), jnp.float32)

    def grant(mib):
        return pltpu.CompilerParams(vmem_limit_bytes=mib * 1024 * 1024)

    params = grant(10)
    dims = (rows_here, group, wide, core)
    early, far = messages[: group + near], messages[group + near :]
    x, y, weight, start, *sums = pl.pallas_call(
        functools.partial(near_kernel, dims),
        out_shape=(field_buffer,) * 3
        + (tile,)
        + (square,) * 4,
        in_specs=[smem] + [vmem] * len(early),
        out_specs=[vmem] * 8,
        scratch_shapes=[
            pltpu.VMEM((2 * rows_here * len(early), LANES), jnp.float32),
            pltpu.VMEM((tall // 2, core, nm), jnp.float32),
        ],
        compiler_params=params,
        cost_estimate=pl.CostEstimate(flops=10**9, bytes_accessed=4 * 10**7, transcendentals=0),
        name="near",
    )(place, *early)
    n_far = len(far)
    back_block = jax.ShapeDtypeStruct((rows_here * core + tall, nm), jnp.float32)
    packed = jax.ShapeDtypeStruct((3 * nm // 2, nm), jnp.float32)
    _, _, _, packed, ray, coup, field, row0, *back = pl.pallas_call(
        functools.partial(far_kernel, dims),
        out_shape=(field_buffer,) * 3
        + (packed,)
        + (square,) * 2
        + (tile, jax.ShapeDtypeStruct((core, nm), jnp.float32))
        + (back_block,) * (group - 1),
        in_specs=[smem] + [vmem] * (n_far + 8),
        out_specs=[vmem] * (7 + group),
        input_output_aliases={1 + n_far + i: i for i in range(3)},
        scratch_shapes=[
            pltpu.VMEM((2 * rows_here * n_far, LANES), jnp.float32),
            pltpu.VMEM((tall // 2, core, nm), jnp.float32),
            pltpu.VMEM((nm, nm), jnp.float32),
            pltpu.VMEM((nm, nm), jnp.float32),
        ],
        compiler_params=params,
        cost_estimate=pl.CostEstimate(flops=10**9, bytes_accessed=2 * 10**7, transcendentals=0),
        name="far",
    )(place, *far, x, y, weight, start, *sums)

    recv = lax.ppermute(field, "cuts", [(i, i + 1) for i in range(cuts - 1)])
    packed, packed_there = sum_over(packed, "rows")
    down = lax.ppermute(row0, "rows", hop(0))
    sent = back
    back = []
    for k in range(1, group):
        back.append(xor_swap(sent[k - 1], "rows", k))

    turned = pl.pallas_call(
        turn_kernel,
        out_shape=jax.ShapeDtypeStruct(rotations.shape[1:], jnp.float32),
        in_specs=[vmem] * 2,
        out_specs=vmem,
        compiler_params=grant(2),
        cost_estimate=pl.CostEstimate(flops=10**8, bytes_accessed=10**6, transcendentals=0),
        name="turn",
    )(rotations[0], ordering[0])
    big = min(nm, 64)
    mix = pl.pallas_call(
        functools.partial(mixing_kernel, 1.0 / pixels),
        out_shape=square,
        in_specs=[vmem] * 3,
        out_specs=vmem,
        compiler_params=grant(4),
        cost_estimate=pl.CostEstimate(flops=10**9, bytes_accessed=4 * 10**7, transcendentals=0),
        scratch_shapes=[
            pltpu.VMEM((nm, nm), jnp.float32),
            pltpu.VMEM((big, nm), jnp.float32),
            pltpu.VMEM((nm, nm), jnp.float32),
        ],
        name="mixing",
    )(packed, packed_there, turned)

    before = lax.ppermute(mix, "cuts", [(i, i + 1) for i in range(cuts - 1)])
    edges = [k for k in range(1, group) if k & (k + 1) == 0]
    beside = [back[k - 1] for k in edges]
    recv, down, beside, mix_now = lax.optimization_barrier((recv, down, beside, mix))
    flip = q == near - 1
    turn = [jnp.where(flip, tall - 1, 0), jnp.where(flip, -1, 1)]
    turn += [(((q ^ (q + 1)) == k) & (q != group - 1)).astype(jnp.int32) for k in edges]
    turn = jnp.stack(turn)
    ray, coup = pl.pallas_call(
        functools.partial(late_kernel, (rows_here, tall, core)),
        out_shape=(square, square),
        in_specs=[smem] + [vmem] * (5 + len(edges)),
        out_specs=[vmem] * 2,
        scratch_shapes=[pltpu.VMEM((tall, nm), jnp.float32)],
        compiler_params=grant(6),
        cost_estimate=pl.CostEstimate(flops=10**9, bytes_accessed=10**7, transcendentals=0),
        name="late",
    )(turn.astype(jnp.int32), field, recv, down, ray, coup, *beside)
    share = nm // peers
    first = (cut == 0).astype(jnp.int32).reshape(1)
    shares = pl.pallas_call(
        functools.partial(project_kernel, peers, 1.0 / pixels),
        out_shape=jax.ShapeDtypeStruct((2 * nm, nm), jnp.float32),
        in_specs=[smem] + [vmem] * 4,
        out_specs=vmem,
        compiler_params=grant(4),
        cost_estimate=pl.CostEstimate(flops=10**8, bytes_accessed=10**6, transcendentals=0),
        name="project",
    )(first, ray, coup, before, mix_now)
    shares = shares.reshape(peers, 2 * share, nm)
    shares = lax.all_to_all(shares, "rows", 0, 0).sum(0)
    coupling, rayleigh = shares[:share], shares[share:]

    where = []
    for k in range(group):
        source = q ^ k
        base = 0
        if k == 0:
            base = jnp.where(lower, q * rows_here, tall - rows_here - q * rows_here)
        down_there = source >= near
        where += [
            source,
            jnp.where(down_there, base, base + rows_here - 1),
            jnp.where(down_there, 1, -1),
        ]
    where = jnp.stack([jnp.asarray(p, jnp.int32) for p in where])
    modes = pl.pallas_call(
        functools.partial(modes_kernel, (rows_here, group, core)),
        out_shape=jax.ShapeDtypeStruct((rows_here, columns, nm), jnp.float32),
        in_specs=[smem] + [vmem] * (group + 1),
        out_specs=hbm,
        scratch_shapes=[
            pltpu.VMEM((rows_here, columns, nm), jnp.float32),
            pltpu.SemaphoreType.DMA((rows_here,)),
        ],
        compiler_params=grant(6),
        cost_estimate=pl.CostEstimate(flops=10**9, bytes_accessed=10**7, transcendentals=0),
        name="modes",
    )(where, field, *back, mix)
    return modes[None], coupling[None], rayleigh[None]


def solution(mesh):
    placed = (
        P("cuts", "rows", None, None),
        P("cuts", "rows", None),
        P("cuts", None, None, None),
        P("cuts", None, None),
    )

    return jax.shard_map(
        body,
        mesh=mesh,
        in_specs=placed,
        out_specs=(P("cuts", "rows", None, None), P("cuts", "rows", None), P("cuts", "rows", None)),
        check_vma=False,
    )
```

```python
import functools

import jax
import jax.numpy as jnp
from jax import lax
from jax.experimental import pallas as pl
from jax.experimental.pallas import tpu as pltpu
from jax.sharding import PartitionSpec as P


DEGREE = 4
ITERS = 2
DEPTH = DEGREE * ITERS
LANES = 128
HIGHEST = lax.Precision.HIGHEST


def mm(a, b):
    return jnp.dot(a, b, precision=HIGHEST, preferred_element_type=jnp.float32)


def mm_t(a, b):
    return lax.dot_general(
        a, b, (((0,), (0,)), ((), ())), precision=HIGHEST, preferred_element_type=jnp.float32
    )


def spread(messages, dims, pos, col, at, sign, x, weight, cs):
    rows_here, wide = dims
    nm = x.shape[2]
    for i, message in enumerate(messages):
        for r in range(rows_here):
            x[pos[at + i] + sign * r, pl.ds(col, wide), :] = message[r * wide : (r + 1) * wide, :]
        cs[2 * rows_here * i : 2 * rows_here * (i + 1), :] = message[rows_here * wide :, :]
    turned = (1.6 * cs[...] - 0.4).T
    for i in range(len(messages)):
        for r in range(rows_here):
            row = pos[at + i] + sign * r
            c = 2 * (rows_here * i + r)
            weight[row, pl.ds(col, LANES), :] = jnp.broadcast_to(
                turned[:, c : c + 1], (LANES, nm)
            )
            weight[row, pl.ds(pl.multiple_of(col + LANES, 8), wide - LANES), :] = (
                jnp.broadcast_to(turned[: wide - LANES, c + 1 : c + 2], (wide - LANES, nm))
            )


def apply_rows(dst, src, weight, wide, sides, first, last, opening):
    left = DEPTH
    at_left, at_right = sides
    count = last - first
    strip = wide // 3 if wide % 24 == 0 else wide
    unroll = 4

    for c0 in range(left, left + wide, strip):
        c1 = c0 + strip

        def row(r, up, ctr, c0=c0, c1=c1):
            down = src[r + 1, c0:c1, :]
            s = (up + down) + (src[r, c0 - 1 : c1 - 1, :] + src[r, c0 + 1 : c1 + 1, :])
            v = weight[r, c0:c1, :] * ctr + 0.4 * s
            if opening:
                v = 0.5 * v
            else:
                v = v - dst[r, c0:c1, :]
            a, b = c0, c1
            if c0 == left:
                edge = v[:DEPTH]
                dst[r, a : a + DEPTH, :] = jnp.where(at_left == 1, jnp.zeros_like(edge), edge)
                v, a = v[DEPTH:], a + DEPTH
            if c1 == left + wide:
                edge = v[b - DEPTH - a :]
                dst[r, b - DEPTH : b, :] = jnp.where(at_right == 1, jnp.zeros_like(edge), edge)
                v, b = v[: b - DEPTH - a], b - DEPTH
            dst[r, a:b, :] = v
            return ctr, down

        def rows(i, pair):
            for j in range(unroll):
                pair = row(first + unroll * i + j, *pair)
            return pair

        pair = (src[first - 1, c0:c1, :], src[first, c0:c1, :])
        whole = count // unroll
        if whole > 1:
            pair = lax.fori_loop(0, whole, rows, pair)
        elif whole:
            pair = rows(0, pair)
        for r in range(first + whole * unroll, last):
            pair = row(r, *pair)


def halves(v):
    high = v.astype(jnp.bfloat16)
    low = (v - high.astype(jnp.float32)).astype(jnp.bfloat16)
    return jnp.concatenate([high, low], axis=1)


def fold(p):
    n, m = p.shape[0] // 2, p.shape[1] // 2
    return (p[:n, :m] + p[n:, m:]) + (p[:n, m:] + p[n:, :m])


def block_rows(buf, at, step, lanes_at, core):
    nm = buf.shape[2]

    def take(first, last):
        rows = buf[at + first * step : at + last * step, lanes_at : lanes_at + core, :]
        return halves(rows.reshape((last - first) * step * core, nm))

    return take


def add_gram(left, *pairs):
    right = jnp.concatenate([r for _, r in pairs], axis=1)
    p = lax.dot_general(
        left, right, (((0,), (0,)), ((), ())), preferred_element_type=jnp.float32
    )
    width = left.shape[1]
    for i, (dst, _) in enumerate(pairs):
        dst[...] += fold(p[:, i * width : (i + 1) * width])


def half_operator(x, weight, tmp, first, last, core):
    nm = x.shape[2]
    c0, c1 = 2 * DEPTH, 2 * DEPTH + core
    spot = lax.broadcasted_iota(jnp.int32, (DEPTH, nm), 0)
    for i in range(first, last):
        r = DEPTH + i
        for a, b in ((c0, c1 - DEPTH), (c1 - DEPTH, c1)):
            side = x[r, a + 1 : b + 1, :]
            if b == c1:
                side = jnp.where(spot == DEPTH - 1, 0.0, side)
            if i:
                side = side + x[r - 1, a:b, :]
            tmp[i - first, a - c0 : b - c0, :] = (
                0.25 * weight[r, a:b, :] * x[r, a:b, :] + 0.2 * side
            )


def finish_sums(x, weight, tmp, start, sums, first, last, core, opens):
    gram, ray, coup = sums
    field = block_rows(x, DEPTH, 1, 2 * DEPTH, core)(first, last)
    half_operator(x, weight, tmp, first, last, core)
    half = block_rows(tmp, 0, 1, 0, core)(0, last - first)
    opening = block_rows(start, 0, 1, 0, core)(first, last)
    add_gram(field, (gram, field), (ray, half), (coup, jnp.where(opens, opening, jnp.zeros_like(opening))))


def near_kernel(dims, pos, *refs):
    rows_here, group, wide, core = dims
    tall = rows_here * group
    known = tall + DEPTH
    n_near = group + group // 2
    at = 2 * group
    messages, refs = refs[:n_near], refs[n_near:]
    x, y, weight, start, gram1, gram2, ray, coup, cs, tmp = refs
    nm = x.shape[2]
    span = wide + 2 * DEPTH
    sign, col = pos[at], pl.multiple_of(pos[at + 1], 8)
    low, sides = pos[at + 2], (pos[at + 4], pos[at + 5])
    zero = jnp.zeros((2 * DEPTH, nm), jnp.float32)

    def clear(r, _):
        for buf in (x, y, weight):
            buf[r, 0 : 2 * DEPTH, :] = zero
            buf[r, span - 2 * DEPTH : span, :] = zero
        return 0

    lax.fori_loop(0, tall + 2 * DEPTH, clear, 0)
    blank = jnp.zeros((span, nm), jnp.float32)
    y[DEPTH - 1] = blank
    y[known] = blank
    spread(messages, (rows_here, wide), pos, col, 0, sign, x, weight, cs)
    for i in range(tall):
        start[i] = x[DEPTH + i, 2 * DEPTH : 2 * DEPTH + core, :]
    for total in (gram1, gram2, ray, coup):
        total[...] = jnp.zeros_like(total)
    take = block_rows(x, DEPTH, rows_here, 2 * DEPTH, core)
    for k in range(1, DEPTH + 1):
        dst, src = (y, x) if k % 2 else (x, y)
        opening = k % DEGREE == 1
        if k < DEPTH:

            @pl.when(low < DEPTH)
            def _(dst=dst, src=src, k=k, opening=opening):
                apply_rows(dst, src, weight, wide, sides, k, DEPTH, opening)

        apply_rows(dst, src, weight, wide, sides, DEPTH, known - k, opening)
        if k == DEGREE:
            f = take(0, group - DEGREE // rows_here)
            add_gram(f, (gram1, f))
    finish_sums(x, weight, tmp, start, (gram2, ray, coup), 0, tall // 2, core, pos[at + 6] == 1)


def far_kernel(dims, pos, *refs):
    rows_here, group, wide, core = dims
    tall = rows_here * group
    known = tall + DEPTH
    n_far = group // 2
    at = 2 * group
    messages, refs = refs[:n_far], refs[n_far:]
    start, gram1_in, gram2_in, ray_in, coup_in, refs = *refs[3:8], refs[8:]
    x, y, weight, packed, ray, coup, out, row0 = refs[:8]
    backs, (cs, tmp, gram1, gram2) = refs[8 : 7 + group], refs[7 + group :]
    sign, col = pos[at], pl.multiple_of(pos[at + 1], 8)
    high, sides = pos[at + 3], (pos[at + 4], pos[at + 5])
    spread(messages, (rows_here, wide), pos, col, group + group // 2, sign, x, weight, cs)
    for total, before in ((gram1, gram1_in), (gram2, gram2_in), (ray, ray_in), (coup, coup_in)):
        total[...] = before[...]
    take = block_rows(x, DEPTH, rows_here, 2 * DEPTH, core)
    for k in range(1, DEPTH + 1):
        dst, src = (y, x) if k % 2 else (x, y)
        opening = k % DEGREE == 1
        apply_rows(dst, src, weight, wide, sides, known - k, known, opening)
        if k < DEPTH:

            @pl.when(high > known)
            def _(dst=dst, src=src, k=k, opening=opening):
                apply_rows(dst, src, weight, wide, sides, known, known + DEPTH - k, opening)

        if k == DEGREE:
            f = take(group - DEGREE // rows_here, group)
            add_gram(f, (gram1, f))
    for i in range(tall):
        out[i] = x[DEPTH + i, 2 * DEPTH : 2 * DEPTH + core, :]
        for back in backs:
            at_end = rows_here * core + i
            back[at_end : at_end + 1, :] = x[DEPTH + i, 2 * DEPTH : 2 * DEPTH + 1, :]
    row0[...] = x[DEPTH + tall - 1, 2 * DEPTH : 2 * DEPTH + core, :]
    for k, back in enumerate(backs):
        for r in range(rows_here):
            back[r * core : (r + 1) * core, :] = x[
                DEPTH + pos[at + 7 + k] + r, 2 * DEPTH : 2 * DEPTH + core, :
            ]
    finish_sums(x, weight, tmp, start, (gram2, ray, coup), tall // 2, tall, core, pos[at + 6] == 1)
    half = gram1.shape[0] // 2
    lane = lax.broadcasted_iota(jnp.int32, (half, 2 * half), 1)
    packed[:half] = gram1[:half]
    packed[half : 2 * half] = gram2[:half]
    packed[2 * half :] = jnp.where(lane < half, pltpu.roll(gram2[half:], half, 1), gram1[half:])


def late_kernel(dims, turn, out, recv, down, ray0, coup0, *refs):
    rows_here, tall, core = dims
    columns, (ray, coup, side) = refs[:-3], refs[-3:]
    coup[...] = coup0[...]
    add_gram(
        block_rows(out, 0, 1, 0, core)(0, tall), (coup, block_rows(recv, 0, 1, 0, core)(0, tall))
    )
    for i in range(tall):
        total = jnp.zeros((1, side.shape[1]), jnp.float32)
        for k, column in enumerate(columns):
            there = column[pl.ds(rows_here * core + turn[0] + turn[1] * i, 1), :]
            total = jnp.where(turn[2 + k] == 1, there, total)
        side[i : i + 1, :] = total
    ray[...] = ray0[...] + 0.2 * (
        mm_t(out[0], down[...]) + mm_t(out[:, core - 1, :], side[...])
    )


def modes_kernel(dims, pos, *refs):
    rows_here, group, core = dims
    blocks, (mix, modes, rows, sem) = refs[:group], refs[group:]
    nm = mix.shape[0]
    m = halves(mix[...])
    m = jnp.concatenate([m, m], axis=0)
    copies = []
    for r in range(rows_here):
        for k in range(group):
            at = pl.multiple_of(pos[3 * k] * core, core)
            row = pos[3 * k + 1] + pos[3 * k + 2] * r
            if k:
                v = blocks[k][pl.ds(pl.multiple_of(row * core, core), core), :]
            else:
                v = blocks[k][row]
            p = jnp.dot(halves(v), m, preferred_element_type=jnp.float32)
            rows[r, pl.ds(at, core), :] = p[:, :nm] + p[:, nm:]
        copies.append(pltpu.make_async_copy(rows.at[r], modes.at[r], sem.at[r]))
        copies[-1].start()
    for c in copies:
        c.wait()


SUB = 8


def inverse_factor(a, work, panel):
    n, big = a.shape[0], panel.shape[0]
    work[...] = a
    full = (SUB, n)
    lane = lax.broadcasted_iota(jnp.int32, full, 1)
    sub = lax.broadcasted_iota(jnp.int32, full, 0)
    for top in range(0, n, big):
        blocks = [work[at : at + SUB, :] for at in range(top, top + big, SUB)]
        for j in range(big // SUB):
            at = top + j * SUB
            diag = blocks[j]
            e = {
                (i, k): jnp.broadcast_to(diag[i : i + 1, at + k : at + k + 1], full)
                for i in range(SUB)
                for k in range(i + 1)
            }
            low, inv = {}, []
            for k in range(SUB):
                inv.append(lax.rsqrt(e[k, k]))
                for i in range(k + 1, SUB):
                    low[i, k] = e[i, k] * inv[k]
                for m in range(k + 1, SUB):
                    for i in range(m, SUB):
                        e[i, m] = e[i, m] - low[i, k] * low[m, k]
            here = (lane >= at) & (lane < at + SUB)
            unit = jnp.where(lane == at + sub, 1.0, 0.0)
            diag = jnp.where(here, unit, diag)
            ups = []
            for k in range(SUB):
                row = jnp.broadcast_to(diag[k : k + 1, :], full)
                for m in range(k):
                    row = row - low[k, m] * ups[m]
                ups.append(row * inv[k])
            done = ups[0]
            for k in range(1, SUB):
                done = jnp.where(sub == k, ups[k], done)
            blocks[j] = done
            for i in range(j + 1, big // SUB):
                cols = []
                for k in range(SUB):
                    c = jnp.broadcast_to(blocks[i][:, at + k : at + k + 1], full)
                    for m in range(k):
                        c = c - low[k, m] * cols[m]
                    cols.append(c * inv[k])
                rest = jnp.where(here, 0.0, blocks[i])
                for k in range(SUB):
                    rest = rest - cols[k] * ups[k]
                blocks[i] = rest
        for j in range(big // SUB):
            at = top + j * SUB
            work[at : at + SUB, :] = blocks[j]
            panel[j * SUB : (j + 1) * SUB, :] = blocks[j]
        if top + big < n:
            done = panel[...]
            r = lax.broadcasted_iota(jnp.int32, done.shape, 0) + top
            c = lax.broadcasted_iota(jnp.int32, done.shape, 1)
            fix = mm_t(done, jnp.where((c > r) & (c < top + big), 0.0, done))
            old = work[top + big :, :]
            spot = lax.broadcasted_iota(jnp.int32, old.shape, 1)
            old = jnp.where((spot >= top) & (spot < top + big), 0.0, old)
            work[top + big :, :] = old - fix[top + big :, :]
    row = lax.broadcasted_iota(jnp.int32, (n, n), 0)
    column = lax.broadcasted_iota(jnp.int32, (n, n), 1)
    work[...] = jnp.where(column <= row, work[...], 0.0)


def turn_kernel(rot, order, turned):
    nm = rot.shape[1]
    ids = lax.broadcasted_iota(jnp.int32, (nm, nm), 0)
    for t in range(rot.shape[0]):
        turned[t] = mm(rot[t], (order[t : t + 1, :] == ids).astype(jnp.float32))


def mixing_kernel(scale, packed, there, turned, mix, work, panel, gram):
    n = mix.shape[0]
    half = n // 2

    def unpack(t):
        at = t * half
        upper = (packed[at : at + half, :] + there[at : at + half, :]) * scale
        rest = (packed[2 * half :, :] + there[2 * half :, :]) * scale
        if t:
            rest = pltpu.roll(rest, half, 1)
        gram[:half, :] = upper
        gram[half:, :] = rest
        gram[half:, :half] = upper.T[half:, :]
        return gram[...]

    inverse_factor(unpack(0), work, panel)
    m1 = mm_t(work[...], turned[0])
    inverse_factor(mm_t(m1, mm(unpack(1), m1)), work, panel)
    m2 = mm_t(work[...], turned[1])
    mix[...] = mm(m1, m2)


def project_kernel(peers, scale, first, ray, coup, before, mix, shares):
    nm = mix.shape[0]
    share = nm // peers
    m = mix[...] * scale

    def place(value, at):
        for r in range(peers):
            to = (2 * ((r % 2) * (peers // 2) + r // 2) + at) * share
            shares[to : to + share, :] = value[r * share : (r + 1) * share, :]

    place(mm_t(mix[...], mm(ray[...] + ray[...].T, m)), 1)
    half = mm_t(coup[...], m)

    @pl.when(first[0] == 1)
    def _():
        place(half, 0)

    @pl.when(first[0] != 1)
    def _():
        place(mm_t(before[...], half), 0)


def xor_swap(value, axis, bit):
    peers = lax.axis_size(axis)
    return lax.ppermute(value, axis, [(i, i ^ bit) for i in range(peers)])


def sum_over(value, axis):
    peers = lax.axis_size(axis)
    bit = 1
    while bit < peers:
        there = xor_swap(value, axis, bit)
        bit *= 2
        if bit < peers:
            value = value + there
    return value, there


def body(start_modes, contrast, rotations, ordering):
    v0, section = start_modes[0], contrast[0]
    rows_here, columns, nm = v0.shape
    peers = lax.axis_size("rows")
    cuts = lax.axis_size("cuts")
    near = DEPTH // rows_here
    group = 2 * near
    core = columns // group
    wide = core + 2 * DEPTH
    tall = group * rows_here
    pixels = rows_here * peers * columns
    me = lax.axis_index("rows")
    cut = lax.axis_index("cuts")
    q = me % group
    block = me // group
    blocks = peers // group

    def hop(j, relayed=False):
        pairs = []
        for i in range(peers):
            z, s = i // group, i % group
            to = z + 1 if (s >= near) != relayed else z - 1
            if 0 <= to < blocks:
                pairs.append((i, to * group + (s ^ j)))
        return pairs

    def window(k):
        at = jnp.clip((q ^ k) * core - DEPTH, 0, columns - wide)
        part = lax.dynamic_slice(v0, (0, at, 0), (rows_here, wide, nm)).reshape(-1, nm)
        tail = lax.dynamic_slice(section, (0, at), (rows_here, wide))
        tail = jnp.pad(tail, ((0, 0), (0, 2 * LANES - wide))).reshape(2 * rows_here, LANES)
        return jnp.concatenate([part, tail], axis=0)

    vmem = pl.BlockSpec(memory_space=pltpu.VMEM)
    smem = pl.BlockSpec(memory_space=pltpu.SMEM)
    hbm = pl.BlockSpec(memory_space=pltpu.HBM)
    windows = [window(k) for k in range(group)]
    arrived = [None] * group
    for k in reversed(range(1, group)):
        arrived[k] = xor_swap(windows[k], "rows", k)
    direct = []
    for j in range(near):
        direct.append(lax.ppermute(windows[j], "rows", hop(j)))
    relay = [lax.ppermute(arrived[k], "rows", hop(0, True)) for k in range(near, group)]
    messages = [windows[0]] + arrived[1:] + direct + relay

    lower = q >= near
    total = tall + 2 * DEPTH
    sign = jnp.where(lower, 1, -1)
    image = [DEPTH + (q ^ k) * rows_here for k in range(group)]
    for j in range(near):
        s = q ^ j
        image.append(jnp.where(lower, (s - near) * rows_here, DEPTH + tall + s * rows_here))
    for k in range(near, group):
        s = q ^ k
        image.append(jnp.where(lower, DEPTH + tall + s * rows_here, (s - near) * rows_here))
    at = jnp.clip(q * core - DEPTH, 0, columns - wide)
    top, bottom = block == 0, block == blocks - 1
    no_near = jnp.where(lower, top, bottom)
    no_far = jnp.where(lower, bottom, top)
    place = [jnp.where(lower, i, total - 1 - i) for i in image] + [
        sign,
        DEPTH + at - (q * core - DEPTH),
        jnp.where(no_near, DEPTH, 0),
        jnp.where(no_far, DEPTH + tall, total),
        q == 0,
        q == group - 1,
        cut == 0,
    ]
    for k in range(1, group):
        s = (q ^ k) * rows_here
        place.append(jnp.where(lower, s, tall - rows_here - s))
    place = jnp.stack([jnp.asarray(p, jnp.int32) for p in place])

    square = jax.ShapeDtypeStruct((nm, nm), jnp.float32)
    tile = jax.ShapeDtypeStruct((tall, core, nm), jnp.float32)
    span = wide + 2 * DEPTH
    field_buffer = jax.ShapeDtypeStruct((total, span, nm), jnp.float32)

    def grant(mib):
        return pltpu.CompilerParams(vmem_limit_bytes=mib * 1024 * 1024)

    params = grant(10)
    dims = (rows_here, group, wide, core)
    early, far = messages[: group + near], messages[group + near :]
    x, y, weight, start, *sums = pl.pallas_call(
        functools.partial(near_kernel, dims),
        out_shape=(field_buffer,) * 3
        + (tile,)
        + (square,) * 4,
        in_specs=[smem] + [vmem] * len(early),
        out_specs=[vmem] * 8,
        scratch_shapes=[
            pltpu.VMEM((2 * rows_here * len(early), LANES), jnp.float32),
            pltpu.VMEM((tall // 2, core, nm), jnp.float32),
        ],
        compiler_params=params,
        cost_estimate=pl.CostEstimate(flops=10**9, bytes_accessed=4 * 10**7, transcendentals=0),
        name="near",
    )(place, *early)
    n_far = len(far)
    back_block = jax.ShapeDtypeStruct((rows_here * core + tall, nm), jnp.float32)
    packed = jax.ShapeDtypeStruct((3 * nm // 2, nm), jnp.float32)
    _, _, _, packed, ray, coup, field, row0, *back = pl.pallas_call(
        functools.partial(far_kernel, dims),
        out_shape=(field_buffer,) * 3
        + (packed,)
        + (square,) * 2
        + (tile, jax.ShapeDtypeStruct((core, nm), jnp.float32))
        + (back_block,) * (group - 1),
        in_specs=[smem] + [vmem] * (n_far + 8),
        out_specs=[vmem] * (7 + group),
        input_output_aliases={1 + n_far + i: i for i in range(3)},
        scratch_shapes=[
            pltpu.VMEM((2 * rows_here * n_far, LANES), jnp.float32),
            pltpu.VMEM((tall // 2, core, nm), jnp.float32),
            pltpu.VMEM((nm, nm), jnp.float32),
            pltpu.VMEM((nm, nm), jnp.float32),
        ],
        compiler_params=params,
        cost_estimate=pl.CostEstimate(flops=10**9, bytes_accessed=2 * 10**7, transcendentals=0),
        name="far",
    )(place, *far, x, y, weight, start, *sums)

    recv = lax.ppermute(field, "cuts", [(i, i + 1) for i in range(cuts - 1)])
    packed, packed_there = sum_over(packed, "rows")
    down = lax.ppermute(row0, "rows", hop(0))
    sent = back
    back = []
    for k in range(1, group):
        back.append(xor_swap(sent[k - 1], "rows", k))

    turned = pl.pallas_call(
        turn_kernel,
        out_shape=jax.ShapeDtypeStruct(rotations.shape[1:], jnp.float32),
        in_specs=[vmem] * 2,
        out_specs=vmem,
        compiler_params=grant(2),
        cost_estimate=pl.CostEstimate(flops=10**8, bytes_accessed=10**6, transcendentals=0),
        name="turn",
    )(rotations[0], ordering[0])
    big = min(nm, 64)
    mix = pl.pallas_call(
        functools.partial(mixing_kernel, 1.0 / pixels),
        out_shape=square,
        in_specs=[vmem] * 3,
        out_specs=vmem,
        compiler_params=grant(4),
        cost_estimate=pl.CostEstimate(flops=10**9, bytes_accessed=4 * 10**7, transcendentals=0),
        scratch_shapes=[
            pltpu.VMEM((nm, nm), jnp.float32),
            pltpu.VMEM((big, nm), jnp.float32),
            pltpu.VMEM((nm, nm), jnp.float32),
        ],
        name="mixing",
    )(packed, packed_there, turned)

    before = lax.ppermute(mix, "cuts", [(i, i + 1) for i in range(cuts - 1)])
    edges = [k for k in range(1, group) if k & (k + 1) == 0]
    beside = [back[k - 1] for k in edges]
    recv, down, beside, mix_now = lax.optimization_barrier((recv, down, beside, mix))
    flip = q == near - 1
    turn = [jnp.where(flip, tall - 1, 0), jnp.where(flip, -1, 1)]
    turn += [(((q ^ (q + 1)) == k) & (q != group - 1)).astype(jnp.int32) for k in edges]
    turn = jnp.stack(turn)
    ray, coup = pl.pallas_call(
        functools.partial(late_kernel, (rows_here, tall, core)),
        out_shape=(square, square),
        in_specs=[smem] + [vmem] * (5 + len(edges)),
        out_specs=[vmem] * 2,
        scratch_shapes=[pltpu.VMEM((tall, nm), jnp.float32)],
        compiler_params=grant(6),
        cost_estimate=pl.CostEstimate(flops=10**9, bytes_accessed=10**7, transcendentals=0),
        name="late",
    )(turn.astype(jnp.int32), field, recv, down, ray, coup, *beside)
    share = nm // peers
    first = (cut == 0).astype(jnp.int32).reshape(1)
    shares = pl.pallas_call(
        functools.partial(project_kernel, peers, 1.0 / pixels),
        out_shape=jax.ShapeDtypeStruct((2 * nm, nm), jnp.float32),
        in_specs=[smem] + [vmem] * 4,
        out_specs=vmem,
        compiler_params=grant(4),
        cost_estimate=pl.CostEstimate(flops=10**8, bytes_accessed=10**6, transcendentals=0),
        name="project",
    )(first, ray, coup, before, mix_now)
    shares = shares.reshape(2, peers // 2, 2 * share, nm)
    odd = (me & 1) == 1
    there = xor_swap(jnp.where(odd, shares[0], shares[1]), "rows", 1)
    shares = jnp.where(odd, shares[1], shares[0]) + there
    sets = [list(range(bit, peers, 2)) for bit in range(2)]
    shares = lax.all_to_all(shares, "rows", 0, 0, axis_index_groups=sets).sum(0)
    coupling, rayleigh = shares[:share], shares[share:]

    where = []
    for k in range(group):
        source = q ^ k
        base = 0
        if k == 0:
            base = jnp.where(lower, q * rows_here, tall - rows_here - q * rows_here)
        down_there = source >= near
        where += [
            source,
            jnp.where(down_there, base, base + rows_here - 1),
            jnp.where(down_there, 1, -1),
        ]
    where = jnp.stack([jnp.asarray(p, jnp.int32) for p in where])
    modes = pl.pallas_call(
        functools.partial(modes_kernel, (rows_here, group, core)),
        out_shape=jax.ShapeDtypeStruct((rows_here, columns, nm), jnp.float32),
        in_specs=[smem] + [vmem] * (group + 1),
        out_specs=hbm,
        scratch_shapes=[
            pltpu.VMEM((rows_here, columns, nm), jnp.float32),
            pltpu.SemaphoreType.DMA((rows_here,)),
        ],
        compiler_params=grant(6),
        cost_estimate=pl.CostEstimate(flops=10**9, bytes_accessed=10**7, transcendentals=0),
        name="modes",
    )(where, field, *back, mix)
    return modes[None], coupling[None], rayleigh[None]


def solution(mesh):
    placed = (
        P("cuts", "rows", None, None),
        P("cuts", "rows", None),
        P("cuts", None, None, None),
        P("cuts", None, None),
    )

    return jax.shard_map(
        body,
        mesh=mesh,
        in_specs=placed,
        out_specs=(P("cuts", "rows", None, None), P("cuts", "rows", None), P("cuts", "rows", None)),
        check_vma=False,
    )
```
